512 devices in a mesh: shard: 64 (over z, y_lo, core), rep: 8 (over x, y_hi).
Axes of the slice: x: 4, y: 8 (y_hi: 2, y_lo: 4; y = y_hi * 4 + y_lo), z: 8, core: 2. Of those that a mesh axis runs over, the one named last changes fastest.
Arguments:
- entity: float32 [65536, 256], P(('shard', 'rep')), may hold values from -1.5 to 1.5
- rel_weight: float32 [900, 256], replicated, may hold values from -4 to 4
- tile_rel: int32 [16384], P(('shard', 'rep')), may hold values from 0 to 899
- tile_head: int32 [16384], P(('shard', 'rep')), may hold values from 0 to 7
- tile_tail: int32 [16384], P(('shard', 'rep')), may hold values from 0 to 7
- tile_mask: int32 [16384, 128, 128], P(('shard', 'rep')), may hold values 0 or 1
- negatives: int32 [16384, 256], P(('shard', 'rep')), may hold values from 0 to 1023
- tile_count: int32 [512], P(('shard', 'rep')), may hold values from 1 to 32, as said below
Outputs:
- entity_grad: float32 [65536, 256], P(('shard', 'rep'))
- rel_grad: float32 [900, 256], replicated
The draws below stay inside these ranges and needn't reach their ends.
Inputs may be any that keep to these rules, and one draw needn't show every extreme that they name: `tile_count`: the used slots of a device are its first ones; some device uses all 32.
All inputs are finite; a program needn't handle non-finite values. No bound on the sum of `tile_mask` on one device may be relied on, other than what follows from the above.
Results may differ from the reference program's by a relative error of at most 0.0003.
Values sent between devices are 32-bit elements; how exact they have to be, the bound alone decides.
A program may use at most 64 MiB of HBM per device.

```python
import jax
import jax.numpy as jnp
from jax import lax

D = 256
RELS = 900
BLOCK = 128
TILES_DEV = 32
NEG = 256
PART = 1024
BLOCKS = 8
ENTITIES = 65536
TILES = 16384
N_SHARD = 64
N_REP = 8


def draw_tile_count(key, part):
    total = N_SHARD * N_REP
    counts = jax.random.randint(jax.random.fold_in(key, 11), (total,), 1, TILES_DEV + 1)
    fullest = jax.random.randint(jax.random.fold_in(key, 12), (), 0, total)
    return counts.at[fullest].set(TILES_DEV).astype(jnp.int32)


def plant(values, stream_key, low, top_value):
    dims = values.shape
    place = [jax.random.randint(jax.random.fold_in(stream_key, axis), (), 0, dims[axis]) for axis in range(len(dims))]
    values = values.at[tuple(place)].set(low)
    longest = dims.index(max(dims))
    place[longest] = (place[longest] + 1) % dims[longest]
    return values.at[tuple(place)].set(top_value)


def shard_levels(rng, shape, shards, least, top_value):
    def one(axis_at, blocks):
        steps = jax.random.uniform(jax.random.fold_in(jax.random.fold_in(rng, 6), axis_at), (blocks,), jnp.float32, least / len(shards), top_value / len(shards))
        return jnp.repeat(jnp.exp(steps), shape[axis_at] // blocks).reshape((-1,) + (1,) * (len(shape) - axis_at - 1))

    level = one(*shards[0])
    for cut in shards[1:]:
        level = level * one(*cut)
    return level


def centred(rng, dims, width, most, shards=(), kind=jnp.bfloat16):
    result = jax.random.normal(rng, dims, jnp.float32) * width
    if len(shards) > 0:
        result = shard_levels(rng, dims, shards, -0.22, 0.18) * result
    return jnp.clip(result, min=-most, max=most).astype(kind)


def setup_inputs(seed: int = 0) -> dict:
    splits = jax.random.split(jax.random.key(seed), 9)
    return {
        "entity": centred(splits[0], (ENTITIES, D), 0.25, 1.5, ((0, 512),), jnp.float32),
        "rel_weight": centred(splits[1], (RELS, D), 1.0, 4.0, (), jnp.float32),
        "tile_rel": plant(jax.random.randint(splits[2], (TILES,), 0, RELS), jax.random.fold_in(splits[2], 1), 0, RELS - 1).astype(jnp.int32),
        "tile_head": plant(jax.random.randint(splits[3], (TILES,), 0, BLOCKS), jax.random.fold_in(splits[3], 1), 0, BLOCKS - 1).astype(jnp.int32),
        "tile_tail": plant(jax.random.randint(splits[4], (TILES,), 0, BLOCKS), jax.random.fold_in(splits[4], 1), 0, BLOCKS - 1).astype(jnp.int32),
        "tile_mask": plant((jax.random.randint(splits[5], (TILES, BLOCK, BLOCK), 0, 16) < 1).astype(jnp.int32), jax.random.fold_in(splits[5], 1), 0, 1),
        "negatives": plant(jax.random.randint(splits[6], (TILES, NEG), 0, PART), jax.random.fold_in(splits[6], 1), 0, PART - 1).astype(jnp.int32),
        "tile_count": draw_tile_count(jax.random.fold_in(splits[8], 71), 0),
    }


def device_terms(head, tail, rel_weight, rels, heads, tails, masks, negs, count):
    high = lax.Precision.HIGHEST
    blocks = head.shape[0] // BLOCK
    head_b = head.reshape(blocks, BLOCK, D)
    tail_b = tail.reshape(blocks, BLOCK, D)
    hrows = head_b[heads]
    trows = tail_b[tails]
    weights = rel_weight[rels]
    nrows = tail[negs]
    live = (jnp.arange(rels.shape[0], dtype=jnp.int32) < count).astype(jnp.float32)
    scaled = hrows * weights[:, None, :]
    scores = jnp.einsum("tik,tjk->tij", scaled, trows, precision=high)
    grads = -(masks.astype(jnp.float32) * live[:, None, None]) * jax.nn.sigmoid(-scores)
    negsc = jnp.einsum("tik,tjk->tij", scaled, nrows, precision=high)
    ngrads = live[:, None, None] * jax.nn.sigmoid(negsc)
    mixed = jnp.einsum("tij,tjk->tik", grads, trows, precision=high) + jnp.einsum("tij,tjk->tik", ngrads, nrows, precision=high)
    dhead = mixed * weights[:, None, :]
    dtail = jnp.einsum("tij,tik->tjk", grads, scaled, precision=high)
    dneg = jnp.einsum("tij,tik->tjk", ngrads, scaled, precision=high)
    dweight = jnp.sum(hrows * mixed, axis=1)
    head_grad = jnp.zeros((blocks, BLOCK, D), jnp.float32).at[heads].add(dhead).reshape(-1, D)
    tail_grad = jnp.zeros((blocks, BLOCK, D), jnp.float32).at[tails].add(dtail).reshape(-1, D)
    tail_grad = tail_grad.at[negs.reshape(-1)].add(dneg.reshape(-1, D))
    rel_grad = jnp.zeros((RELS, D), jnp.float32).at[rels].add(dweight)
    return head_grad, tail_grad, rel_grad


def reference(entity, rel_weight, tile_rel, tile_head, tile_tail, tile_mask, negatives, tile_count):
    parts = entity.reshape(N_SHARD, PART, D)
    rels = tile_rel.reshape(N_SHARD, N_REP, TILES_DEV)
    heads = tile_head.reshape(N_SHARD, N_REP, TILES_DEV)
    tails = tile_tail.reshape(N_SHARD, N_REP, TILES_DEV)
    masks = tile_mask.reshape(N_SHARD, N_REP, TILES_DEV, BLOCK, BLOCK)
    negs = negatives.reshape(N_SHARD, N_REP, TILES_DEV, NEG)
    counts = tile_count.reshape(N_SHARD, N_REP)

    def per_shard(carry, index):
        grads, rel_total = carry
        lower = (index + N_SHARD - 1) % N_SHARD
        head = parts[index]
        tail = parts[lower]
        terms = jax.vmap(lambda a, b, c, m, n, k: device_terms(head, tail, rel_weight, a, b, c, m, n, k))(
            rels[index], heads[index], tails[index], masks[index], negs[index], counts[index])
        grads = grads.at[index].add(jnp.sum(terms[0], axis=0))
        grads = grads.at[lower].add(jnp.sum(terms[1], axis=0))
        rel_total = rel_total + jnp.sum(terms[2], axis=0)
        return (grads, rel_total), None

    start = (jnp.zeros((N_SHARD, PART, D), jnp.float32), jnp.zeros((RELS, D), jnp.float32))
    (grads, rel_total), unused = lax.scan(per_shard, start, jnp.arange(N_SHARD, dtype=jnp.int32))
    return grads.reshape(ENTITIES, D), rel_total
```

```python
import functools

import jax
import jax.numpy as jnp
from jax import lax
from jax.experimental import pallas as pl
from jax.experimental.pallas import tpu as pltpu
from jax.sharding import PartitionSpec as P

MESH = pl.DeviceIdType.MESH
VMEM = pltpu.VMEM
F32 = jnp.float32
BF16 = jnp.bfloat16
BLOCK = 128
WIDTH = 256
BLOCKS = 8
GROUP = 4
REL_PAD = 1024


def place():
    shard = lax.axis_index("shard")
    rep = lax.axis_index("rep")
    core = shard % 2
    y_lo = (shard // 2) % 4
    z = shard // 8
    x = rep // 2
    y = (rep % 2) * 4 + y_lo
    return x, y, z, core


def device(x, y, z, core):
    x = (x + 8) % 4
    y = (y + 16) % 8
    z = (z + 16) % 8
    return ((z * 4 + y % 4) * 2 + core, x * 2 + y // 4)


def chain(y, z, core, far):
    y_lo = y % 4
    step = 2 * core - 1
    z_step = core * (y_lo // 3) - (1 - core) * ((3 - y_lo) // 3)
    return y + step * (5 if far else 1), z + z_step


def greet(partners):
    barrier = pltpu.get_barrier_semaphore()
    for partner in partners:
        pl.semaphore_signal(barrier, inc=1, device_id=partner, device_id_type=MESH)
    pl.semaphore_wait(barrier, len(partners))


def remote(src, dst, send, recv, target):
    return pltpu.make_async_remote_copy(
        src_ref=src, dst_ref=dst, send_sem=send, recv_sem=recv, device_id=target, device_id_type=MESH
    )


def gather_kernel(own_ref, head, tail, ys, yr, xs, xr, cs, cr, ls):
    x, y, z, core = place()
    q = y // 4
    y_lo = y % 4
    left = device(x - 1, y, z, core)
    right = device(x + 1, y, z, core)
    pair = device(x, y + 4, z, core)
    other = device(x, y, z, 1 - core)
    near = chain(y, z, core, False)
    far = chain(y, z, core, True)
    near_dev = device(x, near[0], near[1], 1 - core)
    far_dev = device(x, far[0], far[1], 1 - core)
    greet([left, right, pair, other, near_dev, far_dev])
    mine = 2 * x + q

    q_near = (q + (3 - y_lo) // 3) % 2
    slots = [(head, q), (head, 1 - q), (tail, q_near), (tail, 1 - q_near)]

    def y_copy(k, target, array):
        return remote(own_ref, array.at[mine], ys.at[k], yr.at[k], target)

    def spread(i, from_own=False):
        array, part = slots[i]
        block = 2 * x + part
        src = own_ref if from_own else array.at[block]
        a = remote(src, array.at[block], xs.at[i, 0], xr.at[i, 0], right)
        b = remote(src, array.at[block], xs.at[i, 1], xr.at[i, 1], left)
        return a, b

    def relay(i):
        array, part = slots[i]
        from_left = 2 * ((x + 3) % 4) + part
        from_right = 2 * ((x + 1) % 4) + part
        half = BLOCK // 2
        top = array.at[from_left, pl.ds(0, half)]
        low = array.at[from_right, pl.ds(half, half)]
        return (
            remote(top, top, xs.at[i, 2], xr.at[i, 2], right),
            remote(low, low, xs.at[i, 3], xr.at[i, 3], left),
        )

    def arrived(i):
        array, part = slots[i]
        from_left = 2 * ((x + 3) % 4) + part
        from_right = 2 * ((x + 1) % 4) + part
        opposite = 2 * ((x + 2) % 4) + part
        half = BLOCK // 2
        l = array.at[from_left]
        r = array.at[from_right]
        t = array.at[opposite, pl.ds(0, half)]
        b = array.at[opposite, pl.ds(half, half)]
        return (
            remote(l, l, xs.at[i, 0], xr.at[i, 0], left),
            remote(r, r, xs.at[i, 1], xr.at[i, 1], right),
            remote(t, t, xs.at[i, 2], xr.at[i, 2], left),
            remote(b, b, xs.at[i, 3], xr.at[i, 3], right),
        )

    def across(block, k, own=False):
        src = own_ref if own else head.at[block]
        return remote(src, tail.at[block], cs.at[k], cr.at[k], other)

    is_head = core == 0
    is_next = core == 1

    @pl.when(is_next)
    def _():
        y_copy(1, near_dev, tail).start()

    y_copy(0, pair, head).start()

    @pl.when(is_next)
    def _():
        y_copy(2, far_dev, tail).start()

    for c in spread(0, True):
        c.start()

    @pl.when(is_head)
    def _():
        across(mine, 0, True).start()

    keep = pltpu.make_async_copy(own_ref, head.at[mine], ls)
    keep.start()

    def pass_on(i, k):
        a, b, _, _ = arrived(i)
        ra, rb = relay(i)
        part = slots[i][1]
        a.wait_recv()
        ra.start()
        if k is not None:
            @pl.when(is_head)
            def _():
                across(2 * ((x + 3) % 4) + part, k).start()
        b.wait_recv()
        rb.start()
        if k is not None:
            @pl.when(is_head)
            def _():
                across(2 * ((x + 1) % 4) + part, k + 1).start()

    def y_arrival(k, array, block):
        return remote(array.at[block], array.at[block], ys.at[k], yr.at[k], pair)

    @pl.when(is_head)
    def _():
        y_arrival(1, tail, 2 * x + q_near).wait_recv()
        for c in spread(2):
            c.start()

    pass_on(0, 1)

    y_arrival(0, head, 2 * x + 1 - q).wait_recv()
    for c in spread(1):
        c.start()

    @pl.when(is_head)
    def _():
        across(2 * x + 1 - q, 3).start()
        pass_on(2, None)
        y_arrival(2, tail, 2 * x + 1 - q_near).wait_recv()
        for c in spread(3):
            c.start()

    pass_on(1, 4)

    def finish(i, k):
        _, _, t, b = arrived(i)
        t.wait_recv()
        b.wait_recv()
        if k is not None:
            @pl.when(is_head)
            def _():
                across(2 * ((x + 2) % 4) + slots[i][1], k).start()

    finish(0, 6)
    finish(1, 7)

    @pl.when(is_head)
    def _():
        pass_on(3, None)
        finish(2, None)
        finish(3, None)

    @pl.when(is_next)
    def _():
        partner_blocks = [
            2 * x + q,
            2 * ((x + 3) % 4) + q,
            2 * ((x + 1) % 4) + q,
            2 * x + 1 - q,
            2 * ((x + 3) % 4) + 1 - q,
            2 * ((x + 1) % 4) + 1 - q,
            2 * ((x + 2) % 4) + q,
            2 * ((x + 2) % 4) + 1 - q,
        ]
        for k, block in enumerate(partner_blocks):
            remote(tail.at[block], tail.at[block], cs.at[k], cr.at[k], other).wait_recv()

    keep.wait()
    y_copy(0, pair, head).wait_send()

    @pl.when(is_next)
    def _():
        y_copy(1, near_dev, tail).wait_send()
        y_copy(2, far_dev, tail).wait_send()

    def sent(i):
        for c in spread(i, i == 0):
            c.wait_send()
        for c in relay(i):
            c.wait_send()

    sent(0)
    sent(1)

    @pl.when(is_head)
    def _():
        sent(2)
        sent(3)
        for k in range(8):
            across(mine, k).wait_send()


def gather(entity):
    out = jax.ShapeDtypeStruct((BLOCKS, BLOCK, WIDTH), F32)
    return pl.pallas_call(
        gather_kernel,
        name="gather_partitions",
        out_shape=(out, out),
        in_specs=[pl.BlockSpec(memory_space=VMEM)],
        out_specs=(pl.BlockSpec(memory_space=VMEM), pl.BlockSpec(memory_space=VMEM)),
        scratch_shapes=[
            pltpu.SemaphoreType.DMA((3,)),
            pltpu.SemaphoreType.DMA((3,)),
            pltpu.SemaphoreType.DMA((4, 4)),
            pltpu.SemaphoreType.DMA((4, 4)),
            pltpu.SemaphoreType.DMA((8,)),
            pltpu.SemaphoreType.DMA((8,)),
            pltpu.SemaphoreType.DMA,
        ],
        compiler_params=pltpu.CompilerParams(collective_id=0, has_side_effects=True, vmem_limit_bytes=32 << 20),
    )(entity)


def halves(value):
    hi = value.astype(BF16)
    lo = (value - hi.astype(F32)).astype(BF16)
    return hi, lo


def dot_nt(a, b):
    return lax.dot_general(a, b, (((1,), (1,)), ((), ())), preferred_element_type=F32)


def terms_kernel(
    rel_s, head_s, tail_s, count_s, head, tail, relw, negs, mask, hgrad, tgrad, rgrad,
    t_cols, t_rows, xx, xt, scores, g_hi, g_lo, mixed, tg_t, counts,
):
    group = pl.program_id(0)
    count = count_s[0]
    parts = 4
    rows = GROUP * BLOCK
    step = WIDTH

    @pl.when(group == 0)
    def _():
        hgrad[...] = jnp.zeros_like(hgrad)
        rgrad[...] = jnp.zeros_like(rgrad)
        tg_t[...] = jnp.zeros_like(tg_t)
        for b in range(BLOCKS):
            hi, lo = halves(tail[b])
            at = pl.ds(b * BLOCK, BLOCK)
            t_cols[at, 0:256] = hi
            t_cols[at, 256:512] = hi
            t_cols[at, 512:768] = lo
            n, sub = b // 2, (b % 2) * BLOCK
            t_rows[n, pl.ds(sub, BLOCK), :] = hi
            t_rows[n, pl.ds(256 + sub, BLOCK), :] = hi
            t_rows[n, pl.ds(512 + sub, BLOCK), :] = lo

    @pl.when(group * GROUP < count)
    def _():
        for j in range(GROUP):
            tile = group * GROUP + j
            at = pl.ds(j * BLOCK, BLOCK)
            scaled = head[head_s[tile]] * relw[pl.ds(rel_s[tile], 1), :]
            hi, lo = halves(scaled)
            xx[at, 0:256] = hi
            xx[at, 256:512] = lo
            xx[at, 512:768] = hi
            hi_t, lo_t = halves(scaled.T)
            xt[:, pl.ds(j * BLOCK, BLOCK)] = hi_t
            xt[:, pl.ds(rows + j * BLOCK, BLOCK)] = lo_t
            xt[:, pl.ds(2 * rows + j * BLOCK, BLOCK)] = hi_t
            live = (tile < count).astype(F32)
            drawn = negs[pl.ds(tile, 1), :]
            upper = (lax.broadcasted_iota(jnp.int32, (BLOCKS, 256), 0) == drawn // BLOCK).astype(F32)
            lower = (lax.broadcasted_iota(jnp.int32, (BLOCK, 256), 0) == drawn % BLOCK).astype(F32)
            counts[j] = dot_nt(upper.astype(BF16), lower.astype(BF16)) * live

        def make_scores(n):
            scores[n] = dot_nt(xx[...], t_cols[pl.ds(n * step, step), :])

        def make_grads(n):
            for j in range(GROUP):
                tile = group * GROUP + j
                alive = tile < count
                at = pl.ds(j * BLOCK, BLOCK)
                marked = mask[j].astype(F32)
                for h in range(2):
                    b = 2 * n + h
                    s = scores[n, at, h * BLOCK:(h + 1) * BLOCK]
                    e = jnp.exp(-jnp.abs(s))
                    big = 1.0 / (1.0 + e)
                    small = e * big
                    up = s >= 0.0
                    here = jnp.where(jnp.logical_and(alive, tail_s[tile] == b), 1.0, 0.0).astype(F32)
                    g = counts[j, b:b + 1, :] * jnp.where(up, big, small) - (marked * here) * jnp.where(up, small, big)
                    hi, lo = halves(g)
                    g_hi[n, at, h * BLOCK:(h + 1) * BLOCK] = hi
                    g_lo[n, at, h * BLOCK:(h + 1) * BLOCK] = lo

        def make_tail(n):
            weights = jnp.concatenate([g_hi[n], g_hi[n], g_lo[n]], axis=0)
            tg_t[:, pl.ds(n * step, step)] += jnp.dot(xt[...], weights, preferred_element_type=F32)

        def make_mixed(n):
            rows_in = jnp.concatenate([g_hi[n], g_lo[n], g_hi[n]], axis=1)
            part = jnp.dot(rows_in, t_rows[n], preferred_element_type=F32)
            if n == 0:
                mixed[...] = part
            else:
                mixed[...] += part

        make_scores(0)
        for n in range(parts):
            if n + 1 < parts:
                make_scores(n + 1)
            make_grads(n)
            make_mixed(n)
            make_tail(n)

        for j in range(GROUP):
            tile = group * GROUP + j
            at = pl.ds(j * BLOCK, BLOCK)
            h, r = head_s[tile], rel_s[tile]
            m = mixed[at, :]
            hgrad[h] += m * relw[pl.ds(r, 1), :]
            row = jnp.sum(head[h] * m, axis=0, keepdims=True)
            rgrad[0, pl.ds(r, 1), :] += row[:, 0:128]
            rgrad[1, pl.ds(r, 1), :] += row[:, 128:256]

    @pl.when(group == pl.num_programs(0) - 1)
    def _():
        for b in range(BLOCKS):
            tgrad[b] = tg_t[:, pl.ds(b * BLOCK, BLOCK)].T


def terms(head, tail, rel_weight, tile_rel, tile_head, tile_tail, tile_mask, negatives, count):
    tiles = tile_mask.shape[0]
    groups = tiles // GROUP
    rows = GROUP * BLOCK
    whole = pl.BlockSpec(memory_space=VMEM)

    def mask_at(g, rel_s, head_s, tail_s, count_s):
        return (jnp.minimum(g, (count_s[0] - 1) // GROUP), 0, 0)

    def fixed(n):
        return lambda g, *_: (0,) * n

    part = jax.ShapeDtypeStruct((BLOCKS, BLOCK, WIDTH), F32)
    return pl.pallas_call(
        terms_kernel,
        name="tile_terms",
        out_shape=(part, part, jax.ShapeDtypeStruct((2, REL_PAD, 128), F32)),
        grid_spec=pltpu.PrefetchScalarGridSpec(
            num_scalar_prefetch=4,
            grid=(groups,),
            in_specs=[
                whole,
                whole,
                whole,
                whole,
                pl.BlockSpec((GROUP, BLOCK, BLOCK), mask_at),
            ],
            out_specs=(whole, whole, whole),
            scratch_shapes=[
                VMEM((BLOCKS * BLOCK, 3 * WIDTH), BF16),
                VMEM((4, 3 * WIDTH, WIDTH), BF16),
                VMEM((rows, 3 * WIDTH), BF16),
                VMEM((WIDTH, 3 * rows), BF16),
                VMEM((4, rows, WIDTH), F32),
                VMEM((4, rows, WIDTH), BF16),
                VMEM((4, rows, WIDTH), BF16),
                VMEM((rows, WIDTH), F32),
                VMEM((WIDTH, BLOCKS * BLOCK), F32),
                VMEM((GROUP, BLOCKS, BLOCK), F32),
            ],
        ),
        compiler_params=pltpu.CompilerParams(dimension_semantics=("arbitrary",), vmem_limit_bytes=48 << 20),
    )(tile_rel, tile_head, tile_tail, count, head, tail, rel_weight, negatives, tile_mask)


def reduce_kernel(
    hg, tg, rg, ent, rel,
    t1, part, opp, fwd, out, fin, ysend, yrecv, rc, r1, rx, r2, ry, r3, rz, full, peer,
    cs, cr, ts, tr, fs, fr, os, orr, ys, yr, rcs, rcr, rxs, rxr, rys, ryr, rzs, rzr, ays, ayr, axs, axr, acs, acr,
):
    x, y, z, core = place()
    q = y // 4
    y_lo = y % 4
    left = device(x - 1, y, z, core)
    right = device(x + 1, y, z, core)
    pair = device(x, y + 4, z, core)
    other = device(x, y, z, 1 - core)
    near = chain(y, z, core, False)
    far = chain(y, z, core, True)
    near_dev = device(x, near[0], near[1], 1 - core)
    far_dev = device(x, far[0], far[1], 1 - core)
    x_peers = [device(x + k, y, z, core) for k in range(1, 4)]
    y_peers = [device(x, y + k, z, core) for k in range(1, 8)]
    z_peers = [device(x, y, z + k, core) for k in range(1, 8)]
    greet(x_peers + y_peers + z_peers + [other, near_dev, far_dev])
    is_head = core == 0
    is_next = core == 1
    half = BLOCK // 2
    q_near = (q + (3 - y_lo) // 3) % 2
    slots = [(part, q), (part, 1 - q), (tg, q_near), (tg, 1 - q_near)]
    x_l, x_r, x_o = (x + 3) % 4, (x + 1) % 4, (x + 2) % 4

    rel_core = remote(rg.at[1 - core], rc, rcs, rcr, other)
    rel_core.start()

    to_other = remote(tg, t1, cs, cr, other)

    @pl.when(is_next)
    def _():
        to_other.start()
        part[...] = hg[...]

    def opposite(i):
        array, p = slots[i]
        block = 2 * x_o + p
        return (
            remote(array.at[block, pl.ds(0, half)], fwd.at[i, 0], fs.at[i, 0], fr.at[i, 0], right),
            remote(array.at[block, pl.ds(half, half)], fwd.at[i, 1], fs.at[i, 1], fr.at[i, 1], left),
        )

    def onward(i):
        return (
            remote(out.at[i, 0], fin.at[i, 0], os.at[i, 0], orr.at[i, 0], right),
            remote(out.at[i, 1], fin.at[i, 1], os.at[i, 1], orr.at[i, 1], left),
        )

    def start_opposite(i):
        for c in opposite(i):
            c.start()

    def add_and_send(i):
        array, p = slots[i]
        a, b = opposite(i)
        to_right, to_left = onward(i)
        a.wait_recv()
        out[i, 0, 0:half, :] = array[2 * x_r + p, 0:half, :] + fwd[i, 0]
        out[i, 0, half:BLOCK, :] = array[2 * x_r + p, half:BLOCK, :]
        to_right.start()
        b.wait_recv()
        out[i, 1, half:BLOCK, :] = array[2 * x_l + p, half:BLOCK, :] + fwd[i, 1]
        out[i, 1, 0:half, :] = array[2 * x_l + p, 0:half, :]
        to_left.start()

    def total(i):
        array, p = slots[i]
        to_right, to_left = onward(i)
        to_right.wait_recv()
        to_left.wait_recv()
        return array[2 * x + p] + fin[i, 0] + fin[i, 1]

    @pl.when(is_head)
    def _():
        start_opposite(2)
        start_opposite(3)

    @pl.when(is_next)
    def _():
        start_opposite(0)
        start_opposite(1)

    rel_core.wait_recv()
    r1[...] = rg[core] + rc[...]

    def rel_x(k):
        to = (x + k) % 4
        return remote(r1.at[pl.ds(pl.multiple_of(to * 256, 256), 256)], rx.at[k - 1], rxs.at[k - 1], rxr.at[k - 1], x_peers[k - 1])

    for k in range(1, 4):
        rel_x(k).start()

    @pl.when(is_head)
    def _():
        to_other.wait_recv()
        part[...] = hg[...] + t1[...]
        start_opposite(0)
        start_opposite(1)
        add_and_send(2)
        add_and_send(3)

    add_and_send(1)
    add_and_send(0)

    for k in range(1, 4):
        rel_x(k).wait_recv()
    r2[...] = r1[pl.ds(pl.multiple_of(x * 256, 256), 256), :] + rx[0] + rx[1] + rx[2]

    def rel_y(k):
        to = (y + k) % 8
        return remote(r2.at[pl.ds(pl.multiple_of(to * 32, 32), 32)], ry.at[k - 1], rys.at[k - 1], ryr.at[k - 1], y_peers[k - 1])

    for k in range(1, 8):
        rel_y(k).start()

    def along_y(k, target):
        return remote(ysend.at[k], yrecv.at[k], ys.at[k], yr.at[k], target)

    @pl.when(is_head)
    def _():
        ysend[1] = total(2)
        along_y(1, near_dev).start()
        ysend[2] = total(3)
        along_y(2, far_dev).start()

    ysend[0] = total(1)
    along_y(0, pair).start()

    for k in range(1, 8):
        rel_y(k).wait_recv()
    acc = r2[pl.ds(pl.multiple_of(y * 32, 32), 32), :]
    for k in range(7):
        acc = acc + ry[k]
    rz[0] = acc
    r3[...] = acc

    def rel_z(k):
        return remote(r3, rz.at[k], rzs.at[k - 1], rzr.at[k - 1], z_peers[k - 1])

    for k in range(1, 8):
        rel_z(k).start()

    ent[...] = total(0)

    for k in range(1, 8):
        rel_z(k).wait_recv()
    acc = rz[z]
    acc = rz[(z + 8) % 8]
    for i in range(1, 8):
        acc = acc + rz[(z - i + 8) % 8]
    chunk = pl.ds(pl.multiple_of(x * 256 + y * 32, 32), 32)
    full[chunk, :] = acc

    def gather_y(k):
        return remote(full.at[chunk], full.at[chunk], ays.at[k - 1], ayr.at[k - 1], y_peers[k - 1])

    def gather_y_in(k):
        src = pl.ds(pl.multiple_of(x * 256 + ((y - k + 8) % 8) * 32, 32), 32)
        return remote(full.at[src], full.at[src], ays.at[k - 1], ayr.at[k - 1], y_peers[k - 1])

    for k in range(1, 8):
        gather_y(k).start()
    for k in range(1, 8):
        gather_y_in(k).wait_recv()

    slab = pl.ds(pl.multiple_of(x * 256, 256), 256)

    def gather_x(k):
        return remote(full.at[slab], full.at[slab], axs.at[k - 1], axr.at[k - 1], x_peers[k - 1])

    def gather_x_in(k):
        src = pl.ds(pl.multiple_of(((x - k + 4) % 4) * 256, 256), 256)
        return remote(full.at[src], full.at[src], axs.at[k - 1], axr.at[k - 1], x_peers[k - 1])

    for k in range(1, 4):
        gather_x(k).start()

    along_y(0, pair).wait_recv()
    ent[...] += yrecv[0]

    @pl.when(is_next)
    def _():
        along_y(1, near_dev).wait_recv()
        along_y(2, far_dev).wait_recv()
        ent[...] += yrecv[1] + yrecv[2]

    for k in range(1, 4):
        gather_x_in(k).wait_recv()

    swap = remote(full, peer, acs, acr, other)
    swap.start()
    n = rel.shape[0]

    @pl.when(is_head)
    def _():
        rel[:, 0:128] = full[0:n, :]

    @pl.when(is_next)
    def _():
        rel[:, 128:256] = full[0:n, :]

    swap.wait_recv()

    @pl.when(is_head)
    def _():
        rel[:, 128:256] = peer[0:n, :]

    @pl.when(is_next)
    def _():
        rel[:, 0:128] = peer[0:n, :]

    swap.wait_send()
    rel_core.wait_send()
    for k in range(1, 4):
        rel_x(k).wait_send()
        gather_x(k).wait_send()
    for k in range(1, 8):
        rel_y(k).wait_send()
        rel_z(k).wait_send()
        gather_y(k).wait_send()

    def sent(i):
        for c in opposite(i):
            c.wait_send()
        for c in onward(i):
            c.wait_send()

    sent(0)
    sent(1)
    along_y(0, pair).wait_send()

    @pl.when(is_head)
    def _():
        sent(2)
        sent(3)
        along_y(1, near_dev).wait_send()
        along_y(2, far_dev).wait_send()

    @pl.when(is_next)
    def _():
        to_other.wait_send()


def reduce(hg, tg, rg, relations):
    whole = pl.BlockSpec(memory_space=VMEM)
    dma = pltpu.SemaphoreType.DMA
    return pl.pallas_call(
        reduce_kernel,
        name="reduce_gradients",
        out_shape=(jax.ShapeDtypeStruct((BLOCK, WIDTH), F32), jax.ShapeDtypeStruct((relations, WIDTH), F32)),
        in_specs=[whole] * 3,
        out_specs=(whole, whole),
        scratch_shapes=[
            VMEM((BLOCKS, BLOCK, WIDTH), F32),
            VMEM((BLOCKS, BLOCK, WIDTH), F32),
            VMEM((8, 128), F32),
            VMEM((4, 2, BLOCK // 2, WIDTH), F32),
            VMEM((4, 2, BLOCK, WIDTH), F32),
            VMEM((4, 2, BLOCK, WIDTH), F32),
            VMEM((3, BLOCK, WIDTH), F32),
            VMEM((3, BLOCK, WIDTH), F32),
            VMEM((REL_PAD, 128), F32),
            VMEM((REL_PAD, 128), F32),
            VMEM((3, 256, 128), F32),
            VMEM((256, 128), F32),
            VMEM((7, 32, 128), F32),
            VMEM((32, 128), F32),
            VMEM((8, 32, 128), F32),
            VMEM((REL_PAD, 128), F32),
            VMEM((REL_PAD, 128), F32),
            dma, dma, dma, dma,
            dma((4, 2)), dma((4, 2)), dma((4, 2)), dma((4, 2)),
            dma((3,)), dma((3,)),
            dma, dma,
            dma((3,)), dma((3,)),
            dma((7,)), dma((7,)),
            dma((7,)), dma((7,)),
            dma((7,)), dma((7,)),
            dma((3,)), dma((3,)),
            dma, dma,
        ],
        compiler_params=pltpu.CompilerParams(collective_id=1, has_side_effects=True, vmem_limit_bytes=40 << 20),
    )(hg, tg, rg)


def local(entity, rel_weight, tile_rel, tile_head, tile_tail, tile_mask, negatives, tile_count):
    head, tail = gather(entity)
    hg, tg, rg = terms(head, tail, rel_weight, tile_rel, tile_head, tile_tail, tile_mask, negatives, tile_count)
    return reduce(hg, tg, rg, rel_weight.shape[0])


def solution(mesh):
    return jax.shard_map(
        local,
        mesh=mesh,
        in_specs=(
            P(("shard", "rep"), None),
            P(),
            P(("shard", "rep")),
            P(("shard", "rep")),
            P(("shard", "rep")),
            P(("shard", "rep"), None, None),
            P(("shard", "rep"), None),
            P(("shard", "rep")),
        ),
        out_specs=(P(("shard", "rep"), None), P()),
        check_vma=False,
    )
```

```python
import functools

import jax
import jax.numpy as jnp
from jax import lax
from jax.experimental import pallas as pl
from jax.experimental.pallas import tpu as pltpu
from jax.sharding import PartitionSpec as P

MESH = pl.DeviceIdType.MESH
VMEM = pltpu.VMEM
F32 = jnp.float32
BF16 = jnp.bfloat16
BLOCK = 128
WIDTH = 256
BLOCKS = 8
GROUP = 8
REL_PAD = 1024


def place():
    shard = lax.axis_index("shard")
    rep = lax.axis_index("rep")
    core = shard % 2
    y_lo = (shard // 2) % 4
    z = shard // 8
    x = rep // 2
    y = (rep % 2) * 4 + y_lo
    return x, y, z, core


def device(x, y, z, core):
    x = (x + 8) % 4
    y = (y + 16) % 8
    z = (z + 16) % 8
    return ((z * 4 + y % 4) * 2 + core, x * 2 + y // 4)


def greet(partners):
    barrier = pltpu.get_barrier_semaphore()
    for partner in partners:
        pl.semaphore_signal(barrier, inc=1, device_id=partner, device_id_type=MESH)
    pl.semaphore_wait(barrier, len(partners))


def remote(src, dst, send, recv, target):
    return pltpu.make_async_remote_copy(
        src_ref=src, dst_ref=dst, send_sem=send, recv_sem=recv, device_id=target, device_id_type=MESH
    )


def gather_kernel(
    own_ref, relw_in, negs_in, mask_in, rel_in, head_in, tail_in,
    head, tail, relw, negs, mask, rel_s, head_s, tail_s,
    ys, yr, xs, xr, cs, cr, ls, ms,
):
    x, y, z, core = place()
    brought = [(relw_in, relw), (negs_in, negs), (mask_in, mask), (rel_in, rel_s), (head_in, head_s), (tail_in, tail_s)]
    local_copies = [pltpu.make_async_copy(src, dst, ms.at[k]) for k, (src, dst) in enumerate(brought)]
    for c in local_copies:
        c.start()
    q = y // 4
    y_lo = y % 4
    pair = device(x, y + 4, z, core)
    other = device(x, y, z, 1 - core)
    x_peers = [device(x + k, y, z, core) for k in range(1, 4)]
    chain_dev = device(x, y + 2 * core - 1, z + core * (y_lo // 3) - (1 - core) * ((3 - y_lo) // 3), 1 - core)
    is_head = core == 0
    is_next = core == 1
    mine = 2 * x + q
    q_near = (q + (3 - y_lo) // 3) % 2
    half = BLOCK // 2
    keep = pltpu.make_async_copy(own_ref, head.at[mine], ls)
    keep.start()
    greet([pair, other, chain_dev] + x_peers)

    streams = [
        (head, q, 0, BLOCK),
        (tail, q_near, 0, BLOCK),
        (head, 1 - q, 0, half),
        (head, 1 - q, half, half),
        (tail, 1 - q_near, 0, half),
        (tail, 1 - q_near, half, half),
    ]

    def piece(i, xx):
        array, part, first, rows = streams[i]
        return array.at[2 * xx + part, pl.ds(first, rows)]

    def along_x(i, k):
        src = own_ref if i == 0 else piece(i, x)
        return remote(src, piece(i, x), xs.at[i, k - 1], xr.at[i, k - 1], x_peers[k - 1])

    def from_x(i, k):
        at = piece(i, (x - k + 4) % 4)
        return remote(at, at, xs.at[i, k - 1], xr.at[i, k - 1], x_peers[k - 1])

    def spread(i):
        for k in (1, 3, 2):
            along_x(i, k).start()

    def pair_copy(h):
        rows = pl.ds(h * half, half)
        return remote(own_ref.at[rows], head.at[mine, rows], ys.at[h], yr.at[h], pair)

    def pair_in(h):
        at = head.at[2 * x + 1 - q, pl.ds(h * half, half)]
        return remote(at, at, ys.at[h], yr.at[h], pair)

    near_copy = remote(own_ref, tail.at[mine], ys.at[2], yr.at[2], chain_dev)
    near_at = tail.at[2 * x + q_near]
    near_in = remote(near_at, near_at, ys.at[2], yr.at[2], chain_dev)

    def far_copy(h):
        at = (2 * x + 1 - q, pl.ds(h * half, half))
        return remote(head.at[at], tail.at[at], ys.at[3 + h], yr.at[3 + h], chain_dev)

    def far_in(h):
        at = tail.at[2 * x + 1 - q_near, pl.ds(h * half, half)]
        return remote(at, at, ys.at[3 + h], yr.at[3 + h], chain_dev)

    shared = [2 * ((x + k) % 4) + part for part in (q, 1 - q) for k in range(4)]

    def across(n):
        src = own_ref if n == 0 else head.at[shared[n]]
        return remote(src, tail.at[shared[n]], cs.at[n], cr.at[n], other)

    def across_in(n):
        return remote(tail.at[shared[n]], tail.at[shared[n]], cs.at[n], cr.at[n], other)

    @pl.when(is_next)
    def _():
        near_copy.start()

    pair_copy(0).start()
    pair_copy(1).start()
    spread(0)

    @pl.when(is_head)
    def _():
        across(0).start()
        near_in.wait_recv()
        spread(1)

    for h in range(2):
        pair_in(h).wait_recv()

        @pl.when(is_next)
        def _():
            far_copy(h).start()

        spread(2 + h)

    @pl.when(is_head)
    def _():
        across(4).start()
        far_in(0).wait_recv()
        spread(4)
        far_in(1).wait_recv()
        spread(5)

    for k in (3, 1, 2):
        from_x(0, (4 - k) % 4).wait_recv()

        @pl.when(is_head)
        def _():
            across(k).start()

    for k in (3, 1, 2):
        from_x(2, (4 - k) % 4).wait_recv()
        from_x(3, (4 - k) % 4).wait_recv()

        @pl.when(is_head)
        def _():
            across(4 + k).start()

    @pl.when(is_head)
    def _():
        for i in (1, 4, 5):
            for k in range(1, 4):
                from_x(i, k).wait_recv()

    @pl.when(is_next)
    def _():
        for n in range(8):
            across_in(n).wait_recv()

    keep.wait()
    for c in local_copies:
        c.wait()
    for h in range(2):
        pair_copy(h).wait_send()
    for i in (0, 2, 3):
        for k in range(1, 4):
            along_x(i, k).wait_send()

    @pl.when(is_head)
    def _():
        for i in (1, 4, 5):
            for k in range(1, 4):
                along_x(i, k).wait_send()
        for n in range(8):
            across(n).wait_send()

    @pl.when(is_next)
    def _():
        near_copy.wait_send()
        far_copy(0).wait_send()
        far_copy(1).wait_send()


def gather(entity, rel_weight, negatives, tile_mask, tile_rel, tile_head, tile_tail):
    hbm = pl.BlockSpec(memory_space=pltpu.HBM)
    whole = pl.BlockSpec(memory_space=VMEM)
    scalars = pl.BlockSpec(memory_space=pltpu.SMEM)
    part = jax.ShapeDtypeStruct((BLOCKS, BLOCK, WIDTH), F32)
    operands = [entity, rel_weight, negatives, tile_mask, tile_rel, tile_head, tile_tail]
    operands = [pltpu.with_memory_space_constraint(a, pltpu.HBM) for a in operands]
    dma = pltpu.SemaphoreType.DMA
    return pl.pallas_call(
        gather_kernel,
        name="gather_partitions",
        out_shape=(part, part, *[jax.ShapeDtypeStruct(a.shape, a.dtype) for a in operands[1:]]),
        in_specs=[hbm] * 7,
        out_specs=(whole, whole, whole, whole, whole, scalars, scalars, scalars),
        scratch_shapes=[dma((5,)), dma((5,)), dma((6, 3)), dma((6, 3)), dma((8,)), dma((8,)), dma, dma((6,))],
        compiler_params=pltpu.CompilerParams(collective_id=0, has_side_effects=True, vmem_limit_bytes=32 << 20),
    )(*operands)


def halves(value):
    hi = value.astype(BF16)
    lo = (value - hi.astype(F32)).astype(BF16)
    return hi, lo


def dot_nt(a, b):
    return lax.dot_general(a, b, (((1,), (1,)), ((), ())), preferred_element_type=F32)


def terms_kernel(
    rel_s, head_s, tail_s, count_s, head, tail, relw, negs, mask, hgrad, tgrad, listed,
    t_cols, t_rows, xx, xt, scores, g_hi, g_lo, mixed, tg_t, counts,
):
    count = count_s[0]
    parts = 4
    rows = GROUP * BLOCK
    step = WIDTH
    tiles = mask.shape[0]

    hgrad[...] = jnp.zeros_like(hgrad)
    listed[...] = jnp.zeros_like(listed)
    tg_t[...] = jnp.zeros_like(tg_t)
    for b in range(BLOCKS):
        hi, lo = halves(tail[b])
        at = pl.ds(b * BLOCK, BLOCK)
        t_cols[at, 0:256] = hi
        t_cols[at, 256:512] = hi
        t_cols[at, 512:768] = lo
        n, sub = b // 2, (b % 2) * BLOCK
        t_rows[n, pl.ds(sub, BLOCK), :] = hi
        t_rows[n, pl.ds(256 + sub, BLOCK), :] = hi
        t_rows[n, pl.ds(512 + sub, BLOCK), :] = lo

    lane = lax.broadcasted_iota(jnp.int32, (8, 128), 1) % tiles
    ids = jnp.zeros((8, 128), F32)
    for tile in range(tiles):
        ids = jnp.where(lane == tile, rel_s[tile].astype(F32), ids)
    for c in range(2):
        listed[c, tiles:tiles + 8, :] = ids

    def do_group(group, carry):
        for j in range(GROUP):
            tile = group * GROUP + j
            at = pl.ds(j * BLOCK, BLOCK)
            scaled = head[head_s[tile]] * relw[pl.ds(rel_s[tile], 1), :]
            hi, lo = halves(scaled)
            xx[at, 0:256] = hi
            xx[at, 256:512] = lo
            xx[at, 512:768] = hi
            hi_t, lo_t = halves(scaled.T)
            xt[:, pl.ds(j * BLOCK, BLOCK)] = hi_t
            xt[:, pl.ds(rows + j * BLOCK, BLOCK)] = lo_t
            xt[:, pl.ds(2 * rows + j * BLOCK, BLOCK)] = hi_t
            live = (tile < count).astype(F32)
            drawn = negs[pl.ds(tile, 1), :]
            upper = (lax.broadcasted_iota(jnp.int32, (BLOCKS, 256), 0) == drawn // BLOCK).astype(F32)
            lower = (lax.broadcasted_iota(jnp.int32, (BLOCK, 256), 0) == drawn % BLOCK).astype(F32)
            counts[j] = dot_nt(upper.astype(BF16), lower.astype(BF16)) * live

        def make_scores(n):
            scores[n] = dot_nt(xx[...], t_cols[pl.ds(n * step, step), :])

        def make_grads(n):
            for j in range(GROUP):
                tile = group * GROUP + j
                alive = tile < count
                at = pl.ds(j * BLOCK, BLOCK)
                marked = mask[tile].astype(F32)
                for h in range(2):
                    b = 2 * n + h
                    s = scores[n, at, h * BLOCK:(h + 1) * BLOCK]
                    e = jnp.exp(-jnp.abs(s))
                    big = 1.0 / (1.0 + e)
                    small = e * big
                    up = s >= 0.0
                    here = jnp.where(jnp.logical_and(alive, tail_s[tile] == b), 1.0, 0.0).astype(F32)
                    g = counts[j, b:b + 1, :] * jnp.where(up, big, small) - (marked * here) * jnp.where(up, small, big)
                    hi, lo = halves(g)
                    g_hi[n, at, h * BLOCK:(h + 1) * BLOCK] = hi
                    g_lo[n, at, h * BLOCK:(h + 1) * BLOCK] = lo

        def make_tail(n):
            weights = jnp.concatenate([g_hi[n], g_hi[n], g_lo[n]], axis=0)
            tg_t[:, pl.ds(n * step, step)] += jnp.dot(xt[...], weights, preferred_element_type=F32)

        def make_mixed(n):
            rows_in = jnp.concatenate([g_hi[n], g_lo[n], g_hi[n]], axis=1)
            part = jnp.dot(rows_in, t_rows[n], preferred_element_type=F32)
            if n == 0:
                mixed[...] = part
            else:
                mixed[...] += part

        make_scores(0)
        for n in range(parts):
            if n + 1 < parts:
                make_scores(n + 1)
            make_grads(n)
            make_mixed(n)
            make_tail(n)

        for j in range(GROUP):
            tile = group * GROUP + j
            at = pl.ds(j * BLOCK, BLOCK)
            h, r = head_s[tile], rel_s[tile]
            m = mixed[at, :]
            hgrad[h] += m * relw[pl.ds(r, 1), :]
            row = jnp.sum(head[h] * m, axis=0, keepdims=True)
            listed[0, pl.ds(tile, 1), :] = row[:, 0:128]
            listed[1, pl.ds(tile, 1), :] = row[:, 128:256]
        return carry

    lax.fori_loop(0, (count + GROUP - 1) // GROUP, do_group, 0)
    for b in range(BLOCKS):
        tgrad[b] = tg_t[:, pl.ds(b * BLOCK, BLOCK)].T


def terms(head, tail, relw, negs, mask, rel_s, head_s, tail_s, count_s):
    rows = GROUP * BLOCK
    tiles = mask.shape[0]
    whole = pl.BlockSpec(memory_space=VMEM)
    scalars = pl.BlockSpec(memory_space=pltpu.SMEM)
    part = jax.ShapeDtypeStruct((BLOCKS, BLOCK, WIDTH), F32)
    return pl.pallas_call(
        terms_kernel,
        name="tile_terms",
        out_shape=(part, part, jax.ShapeDtypeStruct((2, tiles + 8, 128), F32)),
        in_specs=[scalars] * 4 + [whole] * 5,
        out_specs=(whole, whole, whole),
        scratch_shapes=[
            VMEM((BLOCKS * BLOCK, 3 * WIDTH), BF16),
            VMEM((4, 3 * WIDTH, WIDTH), BF16),
            VMEM((rows, 3 * WIDTH), BF16),
            VMEM((WIDTH, 3 * rows), BF16),
            VMEM((4, rows, WIDTH), F32),
            VMEM((4, rows, WIDTH), BF16),
            VMEM((4, rows, WIDTH), BF16),
            VMEM((rows, WIDTH), F32),
            VMEM((WIDTH, BLOCKS * BLOCK), F32),
            VMEM((GROUP, BLOCKS, BLOCK), F32),
        ],
        compiler_params=pltpu.CompilerParams(vmem_limit_bytes=40 << 20),
    )(rel_s, head_s, tail_s, count_s, head, tail, relw, negs, mask)


def reduce_kernel(
    hg, tg, listed, ent, rel,
    lists, tin, out, fin, ysend, yrecv, p, sy, sz, fy, fz, full, peer,
    ls, lr, ts, tr, xs, xr, ps, pr, rys, ryr, rzs, rzr, bys, byr, bzs, bzr, ays, ayr, azs, azr, gxs, gxr, gcs, gcr,
):
    x, y, z, core = place()
    q = y // 4
    pair = device(x, y + 4, z, core)
    other = device(x, y, z, 1 - core)
    x_peers = [device(x + k, y, z, core) for k in range(1, 4)]
    x_over = [device(x + k, y, z, 1 - core) for k in range(1, 4)]
    y_peers = [device(x, y + k, z, core) for k in range(1, 8)]
    z_peers = [device(x, y, z + k, core) for k in range(1, 8)]
    y_lo = y % 4
    down = device(x, y - 1, z - (3 - y_lo) // 3, 1)
    up = device(x, y + 1, z + y_lo // 3, 0)
    is_head = core == 0
    is_next = core == 1
    chain_dev = device(x, y + 2 * core - 1, z + core * (y_lo // 3) - (1 - core) * ((3 - y_lo) // 3), 1 - core)
    greet(x_peers + x_over + y_peers + z_peers + [other, chain_dev])
    me = core * 4 + x
    tiles = listed.shape[1] - 8

    targets = [(x_peers[k - 1], core, k - 1) for k in range(1, 4)]
    targets += [(x_over[k - 1], 1 - core, 2 + k) for k in range(1, 4)]
    targets += [(other, 1 - core, 6)]

    def list_copy(i):
        target, columns, k = targets[i]
        return remote(listed.at[columns], lists.at[me], ls, lr, target)

    for i in range(7):
        list_copy(i).start()
    lists[me] = listed[core]

    def tail_block(i, q_of):
        parity = 1 - q_of if i < 4 else q_of
        return 2 * ((x + 1 + i % 4) % 4) + parity

    q_down = ((y + 7) % 8) // 4

    def tail_copy(i, q_of, target):
        block = tail_block(i, q_of)
        return remote(tg.at[block], tin.at[i], ts.at[i], tr.at[i], target)

    @pl.when(is_head)
    def _():
        for i in range(8):
            tail_copy(i, q_down, down).start()

    @pl.when(is_next)
    def _():
        for i in range(8):
            tail_copy(i, q, other).start()

    seven = remote(lists.at[pl.ds(0, 7)], lists.at[pl.ds(0, 7)], ls, lr, other)
    seven.wait_recv()
    lane = lax.broadcasted_iota(jnp.int32, (1, 128), 1) // tiles
    picked = []
    for g in range(2):
        row = jnp.zeros((1, 128), F32)
        for d in range(4):
            row = jnp.where(lane == d, lists[g * 4 + d, tiles:tiles + 1, :], row)
        picked.append(row)
    ids = jnp.concatenate(picked, axis=1)
    target_row = (lax.broadcasted_iota(jnp.int32, (256, 256), 0) + x * 256).astype(F32)
    chosen = (target_row == ids).astype(F32).astype(BF16)
    rows = jnp.concatenate([lists[d, 0:tiles, :] for d in range(8)], axis=0)
    hi = rows.astype(BF16)
    rest = rows - hi.astype(F32)
    mid = rest.astype(BF16)
    low = (rest - mid.astype(F32)).astype(BF16)
    placed = jnp.dot(chosen, hi, preferred_element_type=F32)
    placed = placed + jnp.dot(chosen, mid, preferred_element_type=F32)
    placed = placed + jnp.dot(chosen, low, preferred_element_type=F32)
    p[...] = placed

    def chunk(k, base=0):
        return pl.ds(pl.multiple_of(base + k * 16, 16), 16)

    def all_of(buffer, send, recv):
        return remote(buffer, buffer, send, recv, other)

    def first_y(k):
        return remote(p.at[chunk((y + k) % 8)], sy.at[k - 1], rys, ryr, y_peers[k - 1])

    def first_z(k):
        return remote(p.at[chunk((z + k) % 8, 128)], sz.at[k - 1], rzs, rzr, z_peers[k - 1])

    for k in range(1, 8):
        first_y(k).start()
        first_z(k).start()

    def tail_in(i):
        return remote(tin.at[i], tin.at[i], ts.at[i], tr.at[i], other)

    def x_copy(i):
        k = i % 4 + 1
        return remote(out.at[i], fin.at[i // 4, k - 1], xs.at[i], xr.at[i], x_peers[k - 1])

    def pass_block(i):
        tail_in(i).wait_recv()
        out[i] = hg[tail_block(i, q)] + tin[i]
        if i % 4 < 3:
            x_copy(i).start()

    def x_total(c):
        acc = out[4 * c + 3]
        for k in range(3):
            x_copy(4 * c + k).wait_recv()
            acc = acc + fin[c, k]
        return acc

    for i in range(4):
        pass_block(i)

    all_of(sy, rys, ryr).wait_recv()
    acc = p[chunk(y), :]
    for k in range(7):
        acc = acc + sy[k]
    fy[0] = acc

    def second_z(k):
        return remote(fy.at[0], fy.at[k], bzs, bzr, z_peers[k - 1])

    for k in range(1, 8):
        second_z(k).start()
    all_of(sz, rzs, rzr).wait_recv()
    acc = p[chunk(z, 128), :]
    for k in range(7):
        acc = acc + sz[k]
    fz[0] = acc

    def second_y(k):
        return remote(fz.at[0], fz.at[k], bys, byr, y_peers[k - 1])

    for k in range(1, 8):
        second_y(k).start()

    pass_block(4)
    pass_block(5)
    ysend[...] = x_total(0)
    along_y = remote(ysend, yrecv, ps, pr, pair)
    along_y.start()
    pass_block(6)
    pass_block(7)

    all_of(fy.at[pl.ds(1, 7)], bzs, bzr).wait_recv()
    acc = fy[(z + 8) % 8]
    for i in range(1, 8):
        acc = acc + fy[(z - i + 8) % 8]
    slab = x * 256
    at_y = pl.ds(pl.multiple_of(slab + y * 16, 16), 16)
    full[at_y, :] = acc

    def third_y(k):
        return remote(full.at[at_y], full.at[at_y], ays.at[k - 1], ayr.at[k - 1], y_peers[k - 1])

    def third_y_in(k):
        src = pl.ds(pl.multiple_of(slab + ((y - k + 8) % 8) * 16, 16), 16)
        return remote(full.at[src], full.at[src], ays.at[k - 1], ayr.at[k - 1], y_peers[k - 1])

    for k in range(1, 8):
        third_y(k).start()
    all_of(fz.at[pl.ds(1, 7)], bys, byr).wait_recv()
    acc = fz[(y + 8) % 8]
    for i in range(1, 8):
        acc = acc + fz[(y - i + 8) % 8]
    at_z = pl.ds(pl.multiple_of(slab + 128 + z * 16, 16), 16)
    full[at_z, :] = acc

    def third_z(k):
        return remote(full.at[at_z], full.at[at_z], azs.at[k - 1], azr.at[k - 1], z_peers[k - 1])

    def third_z_in(k):
        src = pl.ds(pl.multiple_of(slab + 128 + ((z - k + 8) % 8) * 16, 16), 16)
        return remote(full.at[src], full.at[src], azs.at[k - 1], azr.at[k - 1], z_peers[k - 1])

    for k in range(1, 8):
        third_z(k).start()

    def half(xx, h):
        return pl.ds(pl.multiple_of(xx * 256 + h * 128, 128), 128)

    def gather_x(k, h, n):
        at = pl.ds(pl.multiple_of(slab + h * 128 + n * 16, 16), 16)
        return remote(full.at[at], full.at[at], gxs.at[h, k - 1], gxr.at[h, k - 1], x_peers[k - 1])

    def gather_x_all(k, h):
        at = full.at[half((x - k + 4) % 4, h)]
        return remote(at, at, gxs.at[h, k - 1], gxr.at[h, k - 1], x_peers[k - 1])

    def swap(k, h):
        at = half((x - k + 4) % 4, h)
        return remote(full.at[at], peer.at[at], gcs.at[h, k], gcr.at[h, k], other)

    def spread(h, n):
        for k in (1, 3, 2):
            gather_x(k, h, n).start()

    spread(0, y)
    spread(1, z)
    for k in (1, 7, 2, 6, 3, 5, 4):
        third_y_in(k).wait_recv()
        spread(0, (y - k + 8) % 8)
        third_z_in(k).wait_recv()
        spread(1, (z - k + 8) % 8)
    swap(0, 0).start()
    swap(0, 1).start()
    ent[...] = x_total(1)
    along_y.wait_recv()
    ent[...] += yrecv[...]

    for h in range(2):
        for k in range(1, 4):
            gather_x_all(k, h).wait_recv()
            swap(k, h).start()

    n = rel.shape[0]

    @pl.when(is_head)
    def _():
        rel[:, 0:128] = full[0:n, :]

    @pl.when(is_next)
    def _():
        rel[:, 128:256] = full[0:n, :]

    for h in range(2):
        for k in range(4):
            swap(k, h).wait_recv()

    @pl.when(is_head)
    def _():
        rel[:, 128:256] = peer[0:n, :]

    @pl.when(is_next)
    def _():
        rel[:, 0:128] = peer[0:n, :]

    seven.wait_send()
    for i in range(8):
        tail_in(i).wait_send()
        if i % 4 < 3:
            x_copy(i).wait_send()
    for k in range(1, 8):
        third_y(k).wait_send()
        third_z(k).wait_send()
    all_of(sy, rys, ryr).wait_send()
    all_of(sz, rzs, rzr).wait_send()
    all_of(fy.at[pl.ds(1, 7)], bzs, bzr).wait_send()
    all_of(fz.at[pl.ds(1, 7)], bys, byr).wait_send()
    along_y.wait_send()
    for h in range(2):
        for k in range(1, 4):
            gather_x_all(k, h).wait_send()
        for k in range(4):
            swap(k, h).wait_send()


def reduce(hg, tg, listed, relations):
    whole = pl.BlockSpec(memory_space=VMEM)
    dma = pltpu.SemaphoreType.DMA
    rows = listed.shape[1]
    return pl.pallas_call(
        reduce_kernel,
        name="reduce_gradients",
        out_shape=(jax.ShapeDtypeStruct((BLOCK, WIDTH), F32), jax.ShapeDtypeStruct((relations, WIDTH), F32)),
        in_specs=[whole] * 3,
        out_specs=(whole, whole),
        scratch_shapes=[
            VMEM((8, rows, 128), F32),
            VMEM((BLOCKS, BLOCK, WIDTH), F32),
            VMEM((BLOCKS, BLOCK, WIDTH), F32),
            VMEM((2, 3, BLOCK, WIDTH), F32),
            VMEM((BLOCK, WIDTH), F32),
            VMEM((BLOCK, WIDTH), F32),
            VMEM((256, 128), F32),
            VMEM((7, 16, 128), F32),
            VMEM((7, 16, 128), F32),
            VMEM((8, 16, 128), F32),
            VMEM((8, 16, 128), F32),
            VMEM((REL_PAD, 128), F32),
            VMEM((REL_PAD, 128), F32),
            dma, dma,
            dma((8,)), dma((8,)),
            dma((8,)), dma((8,)),
            dma, dma,
            *[dma] * 8,
            *[dma((7,))] * 4,
            dma((2, 3)), dma((2, 3)),
            dma((2, 4)), dma((2, 4)),
        ],
        compiler_params=pltpu.CompilerParams(collective_id=1, has_side_effects=True, vmem_limit_bytes=40 << 20),
    )(hg, tg, listed)


def local(entity, rel_weight, tile_rel, tile_head, tile_tail, tile_mask, negatives, tile_count):
    ready = gather(entity, rel_weight, negatives, tile_mask, tile_rel, tile_head, tile_tail)
    hg, tg, listed = terms(*ready, tile_count)
    return reduce(hg, tg, listed, rel_weight.shape[0])


def solution(mesh):
    return jax.shard_map(
        local,
        mesh=mesh,
        in_specs=(
            P(("shard", "rep"), None),
            P(),
            P(("shard", "rep")),
            P(("shard", "rep")),
            P(("shard", "rep")),
            P(("shard", "rep"), None, None),
            P(("shard", "rep"), None),
            P(("shard", "rep")),
        ),
        out_specs=(P(("shard", "rep"), None), P()),
        check_vma=False,
    )
```

```python
import functools

import jax
import jax.numpy as jnp
from jax import lax
from jax.experimental import pallas as pl
from jax.experimental.pallas import tpu as pltpu
from jax.sharding import PartitionSpec as P

MESH = pl.DeviceIdType.MESH
VMEM = pltpu.VMEM
F32 = jnp.float32
BF16 = jnp.bfloat16
BLOCK = 128
WIDTH = 256
BLOCKS = 8
GROUP = 8
REL_PAD = 1024


def place():
    shard = lax.axis_index("shard")
    rep = lax.axis_index("rep")
    core = shard % 2
    y_lo = (shard // 2) % 4
    z = shard // 8
    x = rep // 2
    y = (rep % 2) * 4 + y_lo
    return x, y, z, core


def device(x, y, z, core):
    x = (x + 8) % 4
    y = (y + 16) % 8
    z = (z + 16) % 8
    return ((z * 4 + y % 4) * 2 + core, x * 2 + y // 4)


def greet(partners):
    barrier = pltpu.get_barrier_semaphore()
    for partner in partners:
        pl.semaphore_signal(barrier, inc=1, device_id=partner, device_id_type=MESH)
    pl.semaphore_wait(barrier, len(partners))


def remote(src, dst, send, recv, target):
    return pltpu.make_async_remote_copy(
        src_ref=src, dst_ref=dst, send_sem=send, recv_sem=recv, device_id=target, device_id_type=MESH
    )


def halves(value):
    hi = value.astype(BF16)
    lo = (value - hi.astype(F32)).astype(BF16)
    return hi, lo


def gather_kernel(
    own_ref, relw_in, negs_in, mask_in, rel_in, head_in, tail_in,
    head, t_cols, t_rows, relw, negs, mask, rel_s, head_s, tail_s,
    tail, ys, yr, xs, xr, cs, cr, ls, ms,
):
    x, y, z, core = place()
    brought = [(relw_in, relw), (negs_in, negs), (mask_in, mask), (rel_in, rel_s), (head_in, head_s), (tail_in, tail_s)]
    local_copies = [pltpu.make_async_copy(src, dst, ms.at[k]) for k, (src, dst) in enumerate(brought)]
    for c in local_copies:
        c.start()
    q = y // 4
    y_lo = y % 4
    pair = device(x, y + 4, z, core)
    other = device(x, y, z, 1 - core)
    x_peers = [device(x + k, y, z, core) for k in range(1, 4)]
    chain_dev = device(x, y + 2 * core - 1, z + core * (y_lo // 3) - (1 - core) * ((3 - y_lo) // 3), 1 - core)
    is_head = core == 0
    is_next = core == 1
    mine = 2 * x + q
    q_near = (q + (3 - y_lo) // 3) % 2
    half = BLOCK // 2
    keep = pltpu.make_async_copy(own_ref, head.at[mine], ls)
    keep.start()
    greet([pair, other, chain_dev] + x_peers)

    streams = [
        (head, q, 0, BLOCK),
        (tail, q_near, 0, BLOCK),
        (head, 1 - q, 0, half),
        (head, 1 - q, half, half),
        (tail, 1 - q_near, 0, half),
        (tail, 1 - q_near, half, half),
    ]

    def piece(i, xx):
        array, part, first, rows = streams[i]
        return array.at[2 * xx + part, pl.ds(first, rows)]

    def along_x(i, k):
        src = own_ref if i == 0 else piece(i, x)
        return remote(src, piece(i, x), xs.at[i, k - 1], xr.at[i, k - 1], x_peers[k - 1])

    def from_x(i, k):
        at = piece(i, (x - k + 4) % 4)
        return remote(at, at, xs.at[i, k - 1], xr.at[i, k - 1], x_peers[k - 1])

    def spread(i):
        for k in (1, 3, 2):
            along_x(i, k).start()

    def pair_copy(h):
        rows = pl.ds(h * half, half)
        return remote(own_ref.at[rows], head.at[mine, rows], ys.at[h], yr.at[h], pair)

    def pair_in(h):
        at = head.at[2 * x + 1 - q, pl.ds(h * half, half)]
        return remote(at, at, ys.at[h], yr.at[h], pair)

    near_copy = remote(own_ref, tail.at[mine], ys.at[2], yr.at[2], chain_dev)
    near_at = tail.at[2 * x + q_near]
    near_in = remote(near_at, near_at, ys.at[2], yr.at[2], chain_dev)

    def far_copy(h):
        at = (2 * x + 1 - q, pl.ds(h * half, half))
        return remote(head.at[at], tail.at[at], ys.at[3 + h], yr.at[3 + h], chain_dev)

    def far_in(h):
        at = tail.at[2 * x + 1 - q_near, pl.ds(h * half, half)]
        return remote(at, at, ys.at[3 + h], yr.at[3 + h], chain_dev)

    shared = [2 * ((x + k) % 4) + part for part in (q, 1 - q) for k in range(4)]

    def across(n):
        src = own_ref if n == 0 else head.at[shared[n]]
        return remote(src, tail.at[shared[n]], cs.at[n], cr.at[n], other)

    def across_in(n):
        return remote(tail.at[shared[n]], tail.at[shared[n]], cs.at[n], cr.at[n], other)

    def split(block):
        hi, lo = halves(tail[block])
        at = pl.ds(pl.multiple_of(block * BLOCK, BLOCK), BLOCK)
        t_cols[at, 0:256] = hi
        t_cols[at, 256:512] = hi
        t_cols[at, 512:768] = lo
        n, sub = block // 2, (block % 2) * BLOCK
        for k, part in enumerate((hi, hi, lo)):
            t_rows[n, pl.ds(pl.multiple_of(k * 256 + sub, BLOCK), BLOCK), :] = part

    @pl.when(is_next)
    def _():
        near_copy.start()

    pair_copy(0).start()
    pair_copy(1).start()
    spread(0)

    @pl.when(is_head)
    def _():
        across(0).start()
        near_in.wait_recv()
        spread(1)

    for h in range(2):
        pair_in(h).wait_recv()

        @pl.when(is_next)
        def _():
            far_copy(h).start()

        spread(2 + h)

    @pl.when(is_head)
    def _():
        across(4).start()
        far_in(0).wait_recv()
        spread(4)
        far_in(1).wait_recv()
        spread(5)

    for k in (3, 1, 2):
        from_x(0, (4 - k) % 4).wait_recv()

        @pl.when(is_head)
        def _():
            across(k).start()

    for k in (3, 1, 2):
        from_x(2, (4 - k) % 4).wait_recv()
        from_x(3, (4 - k) % 4).wait_recv()

        @pl.when(is_head)
        def _():
            across(4 + k).start()

    @pl.when(is_head)
    def _():
        split(2 * x + q_near)
        split(2 * x + 1 - q_near)
        for k in (1, 3, 2):
            from_x(1, k).wait_recv()
            split(2 * ((x - k + 4) % 4) + q_near)
        for k in (1, 3, 2):
            from_x(4, k).wait_recv()
            from_x(5, k).wait_recv()
            split(2 * ((x - k + 4) % 4) + 1 - q_near)

    @pl.when(is_next)
    def _():
        for n in range(8):
            across_in(n).wait_recv()
            split(shared[n])

    keep.wait()
    for c in local_copies:
        c.wait()
    for h in range(2):
        pair_copy(h).wait_send()
    for i in (0, 2, 3):
        for k in range(1, 4):
            along_x(i, k).wait_send()

    @pl.when(is_head)
    def _():
        for i in (1, 4, 5):
            for k in range(1, 4):
                along_x(i, k).wait_send()
        for n in range(8):
            across(n).wait_send()

    @pl.when(is_next)
    def _():
        near_copy.wait_send()
        far_copy(0).wait_send()
        far_copy(1).wait_send()


def gather(entity, rel_weight, negatives, tile_mask, tile_rel, tile_head, tile_tail):
    hbm = pl.BlockSpec(memory_space=pltpu.HBM)
    whole = pl.BlockSpec(memory_space=VMEM)
    scalars = pl.BlockSpec(memory_space=pltpu.SMEM)
    part = jax.ShapeDtypeStruct((BLOCKS, BLOCK, WIDTH), F32)
    operands = [entity, rel_weight, negatives, tile_mask, tile_rel, tile_head, tile_tail]
    operands = [pltpu.with_memory_space_constraint(a, pltpu.HBM) for a in operands]
    dma = pltpu.SemaphoreType.DMA
    return pl.pallas_call(
        gather_kernel,
        name="gather_partitions",
        out_shape=(
            part,
            jax.ShapeDtypeStruct((BLOCKS * BLOCK, 3 * WIDTH), BF16),
            jax.ShapeDtypeStruct((4, 3 * WIDTH, WIDTH), BF16),
            *[jax.ShapeDtypeStruct(a.shape, a.dtype) for a in operands[1:]],
        ),
        in_specs=[hbm] * 7,
        out_specs=(whole,) * 6 + (scalars,) * 3,
        scratch_shapes=[
            VMEM((BLOCKS, BLOCK, WIDTH), F32),
            dma((5,)), dma((5,)), dma((6, 3)), dma((6, 3)), dma((8,)), dma((8,)), dma, dma((6,)),
        ],
        compiler_params=pltpu.CompilerParams(collective_id=0, has_side_effects=True, vmem_limit_bytes=32 << 20),
    )(*operands)


def dot_nt(a, b):
    return lax.dot_general(a, b, (((1,), (1,)), ((), ())), preferred_element_type=F32)


def terms_kernel(
    rel_s, head_s, tail_s, count_s, head, t_cols, t_rows, relw, negs, mask, hgrad, tgrad, listed,
    xx, xt, scores, g_hi, g_lo, mixed, counts,
):
    count = count_s[0]
    parts = 4
    rows = GROUP * BLOCK
    step = WIDTH
    tiles = mask.shape[0]

    hgrad[...] = jnp.zeros_like(hgrad)
    listed[...] = jnp.zeros_like(listed)
    tgrad[...] = jnp.zeros_like(tgrad)

    lane = lax.broadcasted_iota(jnp.int32, (8, 128), 1) % tiles
    ids = jnp.zeros((8, 128), F32)
    for tile in range(tiles):
        ids = jnp.where(lane == tile, rel_s[tile].astype(F32), ids)
    for c in range(2):
        listed[c, tiles:tiles + 8, :] = ids

    def do_group(group, carry):
        for j in range(GROUP):
            tile = group * GROUP + j
            at = pl.ds(j * BLOCK, BLOCK)
            scaled = head[head_s[tile]] * relw[pl.ds(rel_s[tile], 1), :]
            hi, lo = halves(scaled)
            xx[at, 0:256] = hi
            xx[at, 256:512] = lo
            xx[at, 512:768] = hi
            hi_t, lo_t = halves(scaled.T)
            xt[:, pl.ds(j * BLOCK, BLOCK)] = hi_t
            xt[:, pl.ds(rows + j * BLOCK, BLOCK)] = lo_t
            xt[:, pl.ds(2 * rows + j * BLOCK, BLOCK)] = hi_t
            live = (tile < count).astype(F32)
            drawn = negs[pl.ds(tile, 1), :]
            upper = (lax.broadcasted_iota(jnp.int32, (BLOCKS, 256), 0) == drawn // BLOCK).astype(F32)
            lower = (lax.broadcasted_iota(jnp.int32, (BLOCK, 256), 0) == drawn % BLOCK).astype(F32)
            counts[j] = dot_nt(upper.astype(BF16), lower.astype(BF16)) * live

        def make_scores(n):
            scores[n] = dot_nt(xx[...], t_cols[pl.ds(n * step, step), :])

        def make_grads(n):
            for j in range(GROUP):
                tile = group * GROUP + j
                alive = tile < count
                at = pl.ds(j * BLOCK, BLOCK)
                marked = mask[tile].astype(F32)
                for h in range(2):
                    b = 2 * n + h
                    s = scores[n, at, h * BLOCK:(h + 1) * BLOCK]
                    e = jnp.exp(-jnp.abs(s))
                    big = 1.0 / (1.0 + e)
                    small = e * big
                    up = s >= 0.0
                    here = jnp.where(jnp.logical_and(alive, tail_s[tile] == b), 1.0, 0.0).astype(F32)
                    g = counts[j, b:b + 1, :] * jnp.where(up, big, small) - (marked * here) * jnp.where(up, small, big)
                    hi, lo = halves(g)
                    g_hi[n, at, h * BLOCK:(h + 1) * BLOCK] = hi
                    g_lo[n, at, h * BLOCK:(h + 1) * BLOCK] = lo

        def make_tail(n):
            weights = jnp.concatenate([g_hi[n], g_hi[n], g_lo[n]], axis=0)
            part = jnp.dot(xt[...], weights, preferred_element_type=F32)
            tgrad[n, 0] += part[:, 0:BLOCK]
            tgrad[n, 1] += part[:, BLOCK:]

        def make_mixed(n):
            rows_in = jnp.concatenate([g_hi[n], g_lo[n], g_hi[n]], axis=1)
            part = jnp.dot(rows_in, t_rows[n], preferred_element_type=F32)
            if n == 0:
                mixed[...] = part
            else:
                mixed[...] += part

        make_scores(0)
        for n in range(parts):
            if n + 1 < parts:
                make_scores(n + 1)
            make_grads(n)
            make_mixed(n)
            make_tail(n)

        for j in range(GROUP):
            tile = group * GROUP + j
            at = pl.ds(j * BLOCK, BLOCK)
            h, r = head_s[tile], rel_s[tile]
            m = mixed[at, :]
            hgrad[h] += m * relw[pl.ds(r, 1), :]
            row = jnp.sum(head[h] * m, axis=0, keepdims=True)
            listed[0, pl.ds(tile, 1), :] = row[:, 0:128]
            listed[1, pl.ds(tile, 1), :] = row[:, 128:256]
        return carry

    lax.fori_loop(0, (count + GROUP - 1) // GROUP, do_group, 0)


def terms(head, t_cols, t_rows, relw, negs, mask, rel_s, head_s, tail_s, count_s):
    rows = GROUP * BLOCK
    tiles = mask.shape[0]
    whole = pl.BlockSpec(memory_space=VMEM)
    scalars = pl.BlockSpec(memory_space=pltpu.SMEM)
    part = jax.ShapeDtypeStruct((BLOCKS, BLOCK, WIDTH), F32)
    return pl.pallas_call(
        terms_kernel,
        name="tile_terms",
        out_shape=(part, jax.ShapeDtypeStruct((4, 2, WIDTH, BLOCK), F32), jax.ShapeDtypeStruct((2, tiles + 8, 128), F32)),
        in_specs=[scalars] * 4 + [whole] * 6,
        out_specs=(whole, whole, whole),
        scratch_shapes=[
            VMEM((rows, 3 * WIDTH), BF16),
            VMEM((WIDTH, 3 * rows), BF16),
            VMEM((4, rows, WIDTH), F32),
            VMEM((4, rows, WIDTH), BF16),
            VMEM((4, rows, WIDTH), BF16),
            VMEM((rows, WIDTH), F32),
            VMEM((GROUP, BLOCKS, BLOCK), F32),
        ],
        compiler_params=pltpu.CompilerParams(vmem_limit_bytes=40 << 20),
    )(rel_s, head_s, tail_s, count_s, head, t_cols, t_rows, relw, negs, mask)


def reduce_kernel(
    hg, tg, listed, ent, rel,
    lists, tin, out, fin, tfin, tsend, trecv, ysend, yrecv, p, sz, fz, full, peer,
    ls, lr, ts, tr, xs, xr, us, ur, vs, vr, ps, pr, rzs, rzr, bys, byr, azs, azr, gxs, gxr, gcs, gcr,
):
    x, y, z, core = place()
    q = y // 4
    pair = device(x, y + 4, z, core)
    other = device(x, y, z, 1 - core)
    x_peers = [device(x + k, y, z, core) for k in range(1, 4)]
    x_over = [device(x + k, y, z, 1 - core) for k in range(1, 4)]
    y_peers = [device(x, y + k, z, core) for k in range(1, 8)]
    z_peers = [device(x, y, z + k, core) for k in range(1, 8)]
    y_lo = y % 4
    sign = 2 * core - 1
    z_there = z + core * (y_lo // 3) - (1 - core) * ((3 - y_lo) // 3)
    near_dev = device(x, y + sign, z_there, 1 - core)
    far_dev = device(x, y + 5 * sign, z_there, 1 - core)
    is_head = core == 0
    is_next = core == 1
    greet(x_peers + x_over + y_peers + z_peers + [other, near_dev, far_dev])
    me = core * 4 + x
    tiles = listed.shape[1] - 8

    targets = [(x_peers[k - 1], core, k - 1) for k in range(1, 4)]
    targets += [(x_over[k - 1], 1 - core, 2 + k) for k in range(1, 4)]
    targets += [(other, 1 - core, 6)]

    def list_copy(i):
        target, columns, k = targets[i]
        return remote(listed.at[columns], lists.at[me], ls, lr, target)

    for i in range(7):
        list_copy(i).start()
    lists[me] = listed[core]

    to_other = remote(tg, tin, ts, tr, other)
    q_down = ((y + 7) % 8) // 4

    def tail_x(k):
        return remote(tg.at[(x + k) % 4], tfin.at[k - 1], us.at[k - 1], ur.at[k - 1], x_peers[k - 1])

    def head_block(i):
        return 2 * ((x + 1 + i % 4) % 4) + (1 - q if i < 4 else q)

    def head_x(i, src):
        k = i % 4 + 1
        return remote(src, fin.at[i // 4, k - 1], xs.at[i], xr.at[i], x_peers[k - 1])

    def tail_y(c, target):
        return remote(tsend.at[c], trecv.at[c], vs.at[c], vr.at[c], target)

    sent_blocks = (0, 2, 1, 4, 6, 5)

    @pl.when(is_head)
    def _():
        for k in (1, 3, 2):
            tail_x(k).start()

    @pl.when(is_next)
    def _():
        to_other.start()
        for i in sent_blocks:
            head_x(i, hg.at[head_block(i)]).start()

    seven = remote(lists.at[pl.ds(0, 7)], lists.at[pl.ds(0, 7)], ls, lr, other)
    seven.wait_recv()
    lane = lax.broadcasted_iota(jnp.int32, (1, 128), 1) // tiles
    picked = []
    for g in range(2):
        row = jnp.zeros((1, 128), F32)
        for d in range(4):
            row = jnp.where(lane == d, lists[g * 4 + d, tiles:tiles + 1, :], row)
        picked.append(row)
    ids = jnp.concatenate(picked, axis=1)
    target_row = (lax.broadcasted_iota(jnp.int32, (256, 256), 0) + x * 256).astype(F32)
    chosen = (target_row == ids).astype(F32).astype(BF16)
    rows = jnp.concatenate([lists[d, 0:tiles, :] for d in range(8)], axis=0)
    hi = rows.astype(BF16)
    rest = rows - hi.astype(F32)
    mid = rest.astype(BF16)
    low = (rest - mid.astype(F32)).astype(BF16)
    placed = jnp.dot(chosen, hi, preferred_element_type=F32)
    placed = placed + jnp.dot(chosen, mid, preferred_element_type=F32)
    placed = placed + jnp.dot(chosen, low, preferred_element_type=F32)
    p[...] = placed

    def chunk(k):
        return pl.ds(pl.multiple_of(k * 32, 32), 32)

    def all_of(buffer, send, recv):
        return remote(buffer, buffer, send, recv, other)

    for k in range(1, 8):
        remote(p.at[chunk((z + k) % 8)], sz.at[k - 1], rzs, rzr, z_peers[k - 1]).start()

    @pl.when(is_head)
    def _():
        to_other.wait_recv()
        for i in sent_blocks + (3, 7):
            block = head_block(i)
            out[i] = hg[block] + tin[block // 2, block % 2].T
            if i % 4 < 3:
                head_x(i, out.at[i]).start()

    @pl.when(is_next)
    def _():
        for i in (3, 7):
            out[i] = hg[head_block(i)]

    def x_total(c):
        acc = out[4 * c + 3]
        for k in range(3):
            head_x(4 * c + k, out.at[4 * c + k]).wait_recv()
            acc = acc + fin[c, k]
        return acc

    all_of(sz, rzs, rzr).wait_recv()
    acc = p[chunk(z), :]
    for k in range(7):
        acc = acc + sz[k]
    fz[0] = acc
    for k in range(1, 8):
        remote(fz.at[0], fz.at[k], bys, byr, y_peers[k - 1]).start()

    @pl.when(is_head)
    def _():
        for k in range(1, 4):
            tail_x(k).wait_recv()
        for c, parity in ((0, q_down), (1, 1 - q_down)):
            tsend[c] = tg[x, parity] + tfin[0, parity] + tfin[1, parity] + tfin[2, parity]
        tail_y(0, near_dev).start()
        tail_y(1, far_dev).start()


    all_of(fz.at[pl.ds(1, 7)], bys, byr).wait_recv()
    acc = fz[(y + 8) % 8]
    for i in range(1, 8):
        acc = acc + fz[(y - i + 8) % 8]
    slab = x * 256
    at_z = pl.ds(pl.multiple_of(slab + z * 32, 32), 32)
    full[at_z, :] = acc

    def third_z(k):
        return remote(full.at[at_z], full.at[at_z], azs.at[k - 1], azr.at[k - 1], z_peers[k - 1])

    def third_z_in(k):
        src = pl.ds(pl.multiple_of(slab + ((z - k + 8) % 8) * 32, 32), 32)
        return remote(full.at[src], full.at[src], azs.at[k - 1], azr.at[k - 1], z_peers[k - 1])

    for k in range(1, 8):
        third_z(k).start()

    ysend[...] = x_total(0)
    along_y = remote(ysend, yrecv, ps, pr, pair)
    along_y.start()

    def whole(xx):
        return pl.ds(pl.multiple_of(xx * 256, 256), 256)

    def spread(n):
        at = full.at[pl.ds(pl.multiple_of(slab + n * 32, 32), 32)]
        for k in (1, 3, 2):
            remote(at, at, gxs.at[k - 1], gxr.at[k - 1], x_peers[k - 1]).start()

    def gather_x_all(k):
        at = full.at[whole((x - k + 4) % 4)]
        return remote(at, at, gxs.at[k - 1], gxr.at[k - 1], x_peers[k - 1])

    def swap(k):
        at = whole((x - k + 4) % 4)
        return remote(full.at[at], peer.at[at], gcs.at[k], gcr.at[k], other)

    spread(z)
    for k in (1, 7, 2, 6, 3, 5, 4):
        third_z_in(k).wait_recv()
        spread((z - k + 8) % 8)
    swap(0).start()
    ent[...] = x_total(1)
    along_y.wait_recv()
    ent[...] += yrecv[...]

    @pl.when(is_next)
    def _():
        for c in range(2):
            tail_y(c, near_dev).wait_recv()
        ent[...] += (trecv[0] + trecv[1]).T

    for k in (1, 3, 2):
        gather_x_all(k).wait_recv()
        swap(k).start()

    n = rel.shape[0]

    @pl.when(is_head)
    def _():
        rel[:, 0:128] = full[0:n, :]

    @pl.when(is_next)
    def _():
        rel[:, 128:256] = full[0:n, :]

    for k in range(4):
        swap(k).wait_recv()

    @pl.when(is_head)
    def _():
        rel[:, 128:256] = peer[0:n, :]

    @pl.when(is_next)
    def _():
        rel[:, 0:128] = peer[0:n, :]

    seven.wait_send()
    for i in sent_blocks:
        head_x(i, out.at[i]).wait_send()

    @pl.when(is_head)
    def _():
        for k in range(1, 4):
            tail_x(k).wait_send()
        for c in range(2):
            tail_y(c, near_dev).wait_send()

    @pl.when(is_next)
    def _():
        to_other.wait_send()

    for k in range(1, 8):
        third_z(k).wait_send()
    all_of(sz, rzs, rzr).wait_send()
    all_of(fz.at[pl.ds(1, 7)], bys, byr).wait_send()
    along_y.wait_send()
    for k in range(1, 4):
        gather_x_all(k).wait_send()
    for k in range(4):
        swap(k).wait_send()


def reduce(hg, tg, listed, relations):
    whole = pl.BlockSpec(memory_space=VMEM)
    dma = pltpu.SemaphoreType.DMA
    rows = listed.shape[1]
    return pl.pallas_call(
        reduce_kernel,
        name="reduce_gradients",
        out_shape=(jax.ShapeDtypeStruct((BLOCK, WIDTH), F32), jax.ShapeDtypeStruct((relations, WIDTH), F32)),
        in_specs=[whole] * 3,
        out_specs=(whole, whole),
        scratch_shapes=[
            VMEM((8, rows, 128), F32),
            VMEM((4, 2, WIDTH, BLOCK), F32),
            VMEM((BLOCKS, BLOCK, WIDTH), F32),
            VMEM((2, 3, BLOCK, WIDTH), F32),
            VMEM((3, 2, WIDTH, BLOCK), F32),
            VMEM((2, WIDTH, BLOCK), F32),
            VMEM((2, WIDTH, BLOCK), F32),
            VMEM((BLOCK, WIDTH), F32),
            VMEM((BLOCK, WIDTH), F32),
            VMEM((256, 128), F32),
            VMEM((7, 32, 128), F32),
            VMEM((8, 32, 128), F32),
            VMEM((REL_PAD, 128), F32),
            VMEM((REL_PAD, 128), F32),
            dma, dma,
            dma, dma,
            dma((8,)), dma((8,)),
            dma((3,)), dma((3,)),
            dma((2,)), dma((2,)),
            dma, dma,
            dma, dma, dma, dma,
            dma((7,)), dma((7,)),
            dma((3,)), dma((3,)),
            dma((4,)), dma((4,)),
        ],
        compiler_params=pltpu.CompilerParams(collective_id=1, has_side_effects=True, vmem_limit_bytes=40 << 20),
    )(hg, tg, listed)


def local(entity, rel_weight, tile_rel, tile_head, tile_tail, tile_mask, negatives, tile_count):
    ready = gather(entity, rel_weight, negatives, tile_mask, tile_rel, tile_head, tile_tail)
    hg, tg, listed = terms(*ready, tile_count)
    return reduce(hg, tg, listed, rel_weight.shape[0])


def solution(mesh):
    return jax.shard_map(
        local,
        mesh=mesh,
        in_specs=(
            P(("shard", "rep"), None),
            P(),
            P(("shard", "rep")),
            P(("shard", "rep")),
            P(("shard", "rep")),
            P(("shard", "rep"), None, None),
            P(("shard", "rep"), None),
            P(("shard", "rep")),
        ),
        out_specs=(P(("shard", "rep"), None), P()),
        check_vma=False,
    )
```

```python
import functools

import jax
import jax.numpy as jnp
from jax import lax
from jax.experimental import pallas as pl
from jax.experimental.pallas import tpu as pltpu
from jax.sharding import PartitionSpec as P

MESH = pl.DeviceIdType.MESH
VMEM = pltpu.VMEM
F32 = jnp.float32
BF16 = jnp.bfloat16
BLOCK = 128
WIDTH = 256
BLOCKS = 8
GROUP = 8
REL_PAD = 1024


def place():
    shard = lax.axis_index("shard")
    rep = lax.axis_index("rep")
    core = shard % 2
    y_lo = (shard // 2) % 4
    z = shard // 8
    x = rep // 2
    y = (rep % 2) * 4 + y_lo
    return x, y, z, core


def device(x, y, z, core):
    x = (x + 8) % 4
    y = (y + 16) % 8
    z = (z + 16) % 8
    return ((z * 4 + y % 4) * 2 + core, x * 2 + y // 4)


def greet(partners):
    barrier = pltpu.get_barrier_semaphore()
    for partner in partners:
        pl.semaphore_signal(barrier, inc=1, device_id=partner, device_id_type=MESH)
    pl.semaphore_wait(barrier, len(partners))


def remote(src, dst, send, recv, target):
    return pltpu.make_async_remote_copy(
        src_ref=src, dst_ref=dst, send_sem=send, recv_sem=recv, device_id=target, device_id_type=MESH
    )


def halves(value):
    hi = value.astype(BF16)
    lo = (value - hi.astype(F32)).astype(BF16)
    return hi, lo


def gather_kernel(
    own_ref, relw_in, negs_in, mask_in, rel_in, head_in, tail_in,
    head, t_cols, t_rows, relw, negs, mask, rel_s, head_s, tail_s,
    tail, ys, yr, xs, xr, cs, cr, ls, ms,
):
    x, y, z, core = place()
    brought = [(relw_in, relw), (negs_in, negs), (mask_in, mask), (rel_in, rel_s), (head_in, head_s), (tail_in, tail_s)]
    local_copies = [pltpu.make_async_copy(src, dst, ms.at[k]) for k, (src, dst) in enumerate(brought)]
    for c in local_copies:
        c.start()
    q = y // 4
    y_lo = y % 4
    pair = device(x, y + 4, z, core)
    other = device(x, y, z, 1 - core)
    x_peers = [device(x + k, y, z, core) for k in range(1, 4)]
    chain_dev = device(x, y + 2 * core - 1, z + core * (y_lo // 3) - (1 - core) * ((3 - y_lo) // 3), 1 - core)
    is_head = core == 0
    is_next = core == 1
    mine = 2 * x + q
    q_near = (q + (3 - y_lo) // 3) % 2
    half = BLOCK // 2
    keep = pltpu.make_async_copy(own_ref, head.at[mine], ls)
    keep.start()
    greet([pair, other, chain_dev] + x_peers)

    streams = [
        (head, q, 0, BLOCK),
        (tail, q_near, 0, BLOCK),
        (head, 1 - q, 0, half),
        (head, 1 - q, half, half),
        (tail, 1 - q_near, 0, half),
        (tail, 1 - q_near, half, half),
    ]

    def piece(i, xx):
        array, part, first, rows = streams[i]
        return array.at[2 * xx + part, pl.ds(first, rows)]

    def along_x(i, k):
        src = own_ref if i == 0 else piece(i, x)
        return remote(src, piece(i, x), xs.at[i, k - 1], xr.at[i, k - 1], x_peers[k - 1])

    def from_x(i, k):
        at = piece(i, (x - k + 4) % 4)
        return remote(at, at, xs.at[i, k - 1], xr.at[i, k - 1], x_peers[k - 1])

    def spread(i):
        for k in (1, 3, 2):
            along_x(i, k).start()

    def pair_copy(h):
        rows = pl.ds(h * half, half)
        return remote(own_ref.at[rows], head.at[mine, rows], ys.at[h], yr.at[h], pair)

    def pair_in(h):
        at = head.at[2 * x + 1 - q, pl.ds(h * half, half)]
        return remote(at, at, ys.at[h], yr.at[h], pair)

    near_copy = remote(own_ref, tail.at[mine], ys.at[2], yr.at[2], chain_dev)
    near_at = tail.at[2 * x + q_near]
    near_in = remote(near_at, near_at, ys.at[2], yr.at[2], chain_dev)

    def far_copy(h):
        at = (2 * x + 1 - q, pl.ds(h * half, half))
        return remote(head.at[at], tail.at[at], ys.at[3 + h], yr.at[3 + h], chain_dev)

    def far_in(h):
        at = tail.at[2 * x + 1 - q_near, pl.ds(h * half, half)]
        return remote(at, at, ys.at[3 + h], yr.at[3 + h], chain_dev)

    shared = [2 * ((x + k) % 4) + part for part in (q, 1 - q) for k in range(4)]

    def across(n):
        src = own_ref if n == 0 else head.at[shared[n]]
        return remote(src, tail.at[shared[n]], cs.at[n], cr.at[n], other)

    def across_in(n):
        return remote(tail.at[shared[n]], tail.at[shared[n]], cs.at[n], cr.at[n], other)

    def split(block):
        hi, lo = halves(tail[block])
        at = pl.ds(pl.multiple_of(block * BLOCK, BLOCK), BLOCK)
        t_cols[at, 0:256] = hi
        t_cols[at, 256:512] = hi
        t_cols[at, 512:768] = lo
        n, sub = block // 2, (block % 2) * BLOCK
        for k, part in enumerate((hi, hi, lo)):
            t_rows[n, pl.ds(pl.multiple_of(k * 256 + sub, BLOCK), BLOCK), :] = part

    @pl.when(is_next)
    def _():
        near_copy.start()

    pair_copy(0).start()
    pair_copy(1).start()
    spread(0)

    @pl.when(is_head)
    def _():
        across(0).start()
        near_in.wait_recv()
        spread(1)

    for h in range(2):
        pair_in(h).wait_recv()

        @pl.when(is_next)
        def _():
            far_copy(h).start()

        spread(2 + h)

    @pl.when(is_head)
    def _():
        across(4).start()
        far_in(0).wait_recv()
        spread(4)
        far_in(1).wait_recv()
        spread(5)

    for k in (3, 1, 2):
        from_x(0, (4 - k) % 4).wait_recv()

        @pl.when(is_head)
        def _():
            across(k).start()

    for k in (3, 1, 2):
        from_x(2, (4 - k) % 4).wait_recv()
        from_x(3, (4 - k) % 4).wait_recv()

        @pl.when(is_head)
        def _():
            across(4 + k).start()

    @pl.when(is_head)
    def _():
        split(2 * x + q_near)
        split(2 * x + 1 - q_near)
        for k in (1, 3, 2):
            from_x(1, k).wait_recv()
            split(2 * ((x - k + 4) % 4) + q_near)
        for k in (1, 3, 2):
            from_x(4, k).wait_recv()
            from_x(5, k).wait_recv()
            split(2 * ((x - k + 4) % 4) + 1 - q_near)

    @pl.when(is_next)
    def _():
        for n in range(8):
            across_in(n).wait_recv()
            split(shared[n])

    keep.wait()
    for c in local_copies:
        c.wait()
    for h in range(2):
        pair_copy(h).wait_send()
    for i in (0, 2, 3):
        for k in range(1, 4):
            along_x(i, k).wait_send()

    @pl.when(is_head)
    def _():
        for i in (1, 4, 5):
            for k in range(1, 4):
                along_x(i, k).wait_send()
        for n in range(8):
            across(n).wait_send()

    @pl.when(is_next)
    def _():
        near_copy.wait_send()
        far_copy(0).wait_send()
        far_copy(1).wait_send()


def gather(entity, rel_weight, negatives, tile_mask, tile_rel, tile_head, tile_tail):
    hbm = pl.BlockSpec(memory_space=pltpu.HBM)
    whole = pl.BlockSpec(memory_space=VMEM)
    scalars = pl.BlockSpec(memory_space=pltpu.SMEM)
    part = jax.ShapeDtypeStruct((BLOCKS, BLOCK, WIDTH), F32)
    operands = [entity, rel_weight, negatives, tile_mask, tile_rel, tile_head, tile_tail]
    operands = [pltpu.with_memory_space_constraint(a, pltpu.HBM) for a in operands]
    dma = pltpu.SemaphoreType.DMA
    return pl.pallas_call(
        gather_kernel,
        name="gather_partitions",
        out_shape=(
            part,
            jax.ShapeDtypeStruct((BLOCKS * BLOCK, 3 * WIDTH), BF16),
            jax.ShapeDtypeStruct((4, 3 * WIDTH, WIDTH), BF16),
            *[jax.ShapeDtypeStruct(a.shape, a.dtype) for a in operands[1:]],
        ),
        in_specs=[hbm] * 7,
        out_specs=(whole,) * 6 + (scalars,) * 3,
        scratch_shapes=[
            VMEM((BLOCKS, BLOCK, WIDTH), F32),
            dma((5,)), dma((5,)), dma((6, 3)), dma((6, 3)), dma((8,)), dma((8,)), dma, dma((6,)),
        ],
        compiler_params=pltpu.CompilerParams(collective_id=0, has_side_effects=True, vmem_limit_bytes=32 << 20),
    )(*operands)


def dot_nt(a, b):
    return lax.dot_general(a, b, (((1,), (1,)), ((), ())), preferred_element_type=F32)


def terms_kernel(
    rel_s, head_s, tail_s, count_s, head, t_cols, t_rows, relw, negs, mask, hgrad, listed, xt, g_hi, g_lo,
    xx, scores, mixed, counts, edges,
):
    count = count_s[0]
    parts = 4
    rows = GROUP * BLOCK
    step = WIDTH
    tiles = mask.shape[0]

    hgrad[...] = jnp.zeros_like(hgrad)
    listed[...] = jnp.zeros_like(listed)

    lane = lax.broadcasted_iota(jnp.int32, (8, 128), 1) % tiles
    ids = jnp.zeros((8, 128), F32)
    for tile in range(tiles):
        ids = jnp.where(lane == tile, rel_s[tile].astype(F32), ids)
    for c in range(2):
        listed[c, tiles:tiles + 8, :] = ids

    def do_group(group, carry):
        for j in range(GROUP):
            tile = group * GROUP + j
            at = pl.ds(j * BLOCK, BLOCK)
            scaled = head[head_s[tile]] * relw[pl.ds(rel_s[tile], 1), :]
            hi, lo = halves(scaled)
            xx[at, 0:256] = hi
            xx[at, 256:512] = lo
            xx[at, 512:768] = hi
            hi_t, lo_t = halves(scaled.T)
            xt[group, :, pl.ds(j * BLOCK, BLOCK)] = hi_t
            xt[group, :, pl.ds(rows + j * BLOCK, BLOCK)] = lo_t
            xt[group, :, pl.ds(2 * rows + j * BLOCK, BLOCK)] = hi_t
            live = (tile < count).astype(F32)
            drawn = negs[pl.ds(tile, 1), :]
            upper = (lax.broadcasted_iota(jnp.int32, (BLOCKS, 256), 0) == drawn // BLOCK).astype(F32)
            lower = (lax.broadcasted_iota(jnp.int32, (BLOCK, 256), 0) == drawn % BLOCK).astype(F32)
            counts[j] = dot_nt(upper.astype(BF16), lower.astype(BF16)) * live

        def make_scores(n):
            scores[n] = dot_nt(xx[...], t_cols[pl.ds(n * step, step), :])

        def make_edges(j):
            tile = group * GROUP + j
            b = tail_s[tile]
            at = pl.ds(pl.multiple_of((b % 2) * BLOCK, BLOCK), BLOCK)
            own = scores[b // 2, pl.ds(j * BLOCK, BLOCK), at]
            live = jnp.where(tile < count, 1.0, 0.0).astype(F32)
            edges[j] = (mask[tile].astype(F32) * live) * lax.logistic(-own)

        def make_grads(n):
            for j in range(GROUP):
                tile = group * GROUP + j
                at = pl.ds(j * BLOCK, BLOCK)
                for h in range(2):
                    b = 2 * n + h
                    lanes = slice(h * BLOCK, (h + 1) * BLOCK)
                    here = jnp.where(tail_s[tile] == b, 1.0, 0.0).astype(F32)
                    g = counts[j, b:b + 1, :] * lax.logistic(scores[n, at, lanes]) - here * edges[j]
                    hi, lo = halves(g)
                    g_hi[group, n, at, lanes] = hi
                    g_lo[group, n, at, lanes] = lo

        def make_mixed(n):
            rows_in = jnp.concatenate([g_hi[group, n], g_lo[group, n], g_hi[group, n]], axis=1)
            part = jnp.dot(rows_in, t_rows[n], preferred_element_type=F32)
            if n == 0:
                mixed[...] = part
            else:
                mixed[...] += part

        for n in range(parts):
            make_scores(n)
        for j in range(GROUP):
            make_edges(j)
        for n in range(parts):
            make_grads(n)
            make_mixed(n)

        for j in range(GROUP):
            tile = group * GROUP + j
            at = pl.ds(j * BLOCK, BLOCK)
            h, r = head_s[tile], rel_s[tile]
            m = mixed[at, :]
            hgrad[h] += m * relw[pl.ds(r, 1), :]
            row = jnp.sum(head[h] * m, axis=0, keepdims=True)
            listed[0, pl.ds(tile, 1), :] = row[:, 0:128]
            listed[1, pl.ds(tile, 1), :] = row[:, 128:256]
        return carry

    def no_group(group, carry):
        xt[group] = jnp.zeros(xt.shape[1:], BF16)
        g_hi[group] = jnp.zeros(g_hi.shape[1:], BF16)
        g_lo[group] = jnp.zeros(g_lo.shape[1:], BF16)
        return carry

    used = (count + GROUP - 1) // GROUP
    lax.fori_loop(0, used, do_group, 0)
    lax.fori_loop(used, tiles // GROUP, no_group, 0)


def terms(head, t_cols, t_rows, relw, negs, mask, rel_s, head_s, tail_s, count_s):
    rows = GROUP * BLOCK
    tiles = mask.shape[0]
    whole = pl.BlockSpec(memory_space=VMEM)
    scalars = pl.BlockSpec(memory_space=pltpu.SMEM)
    part = jax.ShapeDtypeStruct((BLOCKS, BLOCK, WIDTH), F32)
    return pl.pallas_call(
        terms_kernel,
        name="tile_terms",
        out_shape=(
            part,
            jax.ShapeDtypeStruct((2, tiles + 8, 128), F32),
            jax.ShapeDtypeStruct((tiles // GROUP, WIDTH, 3 * rows), BF16),
            jax.ShapeDtypeStruct((tiles // GROUP, 4, rows, WIDTH), BF16),
            jax.ShapeDtypeStruct((tiles // GROUP, 4, rows, WIDTH), BF16),
        ),
        in_specs=[scalars] * 4 + [whole] * 6,
        out_specs=(whole,) * 5,
        scratch_shapes=[
            VMEM((rows, 3 * WIDTH), BF16),
            VMEM((4, rows, WIDTH), F32),
            VMEM((rows, WIDTH), F32),
            VMEM((GROUP, BLOCKS, BLOCK), F32),
            VMEM((GROUP, BLOCK, BLOCK), F32),
        ],
        compiler_params=pltpu.CompilerParams(vmem_limit_bytes=16 << 20),
    )(rel_s, head_s, tail_s, count_s, head, t_cols, t_rows, relw, negs, mask)


def reduce_kernel(
    hg, listed, xt, g_hi, g_lo, ent, rel,
    tg, lists, tin, out, fin, tfin, tsend, trecv, ysend, yrecv, p, sz, fz, full, peer,
    ls, lr, ts, tr, xs, xr, us, ur, vs, vr, ps, pr, rzs, rzr, bys, byr, azs, azr, gxs, gxr, gcs, gcr,
):
    x, y, z, core = place()
    q = y // 4
    pair = device(x, y + 4, z, core)
    other = device(x, y, z, 1 - core)
    x_peers = [device(x + k, y, z, core) for k in range(1, 4)]
    x_over = [device(x + k, y, z, 1 - core) for k in range(1, 4)]
    y_peers = [device(x, y + k, z, core) for k in range(1, 8)]
    z_peers = [device(x, y, z + k, core) for k in range(1, 8)]
    y_lo = y % 4
    sign = 2 * core - 1
    z_there = z + core * (y_lo // 3) - (1 - core) * ((3 - y_lo) // 3)
    near_dev = device(x, y + sign, z_there, 1 - core)
    far_dev = device(x, y + 5 * sign, z_there, 1 - core)
    is_head = core == 0
    is_next = core == 1
    partners = x_peers + x_over + y_peers + z_peers + [other, near_dev, far_dev]
    barrier = pltpu.get_barrier_semaphore()
    for partner in partners:
        pl.semaphore_signal(barrier, inc=1, device_id=partner, device_id_type=MESH)

    def tail_products(first):
        def add_group(g, carry):
            for n in (first, first + 1):
                weights = jnp.concatenate([g_hi[g, n], g_hi[g, n], g_lo[g, n]], axis=0)
                products = jnp.dot(xt[g], weights, preferred_element_type=F32)
                tg[n, 0] += products[:, 0:BLOCK]
                tg[n, 1] += products[:, BLOCK:]
            return carry

        for n in (first, first + 1):
            tg[n] = jnp.zeros(tg.shape[1:], F32)
        lax.fori_loop(0, xt.shape[0], add_group, 0)

    tail_products(0)
    pl.semaphore_wait(barrier, len(partners))
    me = core * 4 + x
    tiles = listed.shape[1] - 8

    targets = [(x_peers[k - 1], core, k - 1) for k in range(1, 4)]
    targets += [(x_over[k - 1], 1 - core, 2 + k) for k in range(1, 4)]
    targets += [(other, 1 - core, 6)]

    def list_copy(i):
        target, columns, k = targets[i]
        return remote(listed.at[columns], lists.at[me], ls, lr, target)

    for i in range(7):
        list_copy(i).start()
    lists[me] = listed[core]

    to_other = remote(tg, tin, ts, tr, other)
    q_down = ((y + 7) % 8) // 4

    def tail_x(k):
        return remote(tg.at[(x + k) % 4], tfin.at[k - 1], us.at[k - 1], ur.at[k - 1], x_peers[k - 1])

    def head_block(i):
        return 2 * ((x + 1 + i % 4) % 4) + (1 - q if i < 4 else q)

    def head_x(i, src):
        k = i % 4 + 1
        return remote(src, fin.at[i // 4, k - 1], xs.at[i], xr.at[i], x_peers[k - 1])

    def tail_y(c, target):
        return remote(tsend.at[c], trecv.at[c], vs.at[c], vr.at[c], target)

    sent_blocks = (0, 2, 1, 4, 6, 5)

    @pl.when(is_next)
    def _():
        for i in sent_blocks:
            head_x(i, hg.at[head_block(i)]).start()

    tail_products(2)

    @pl.when(is_head)
    def _():
        for k in (1, 3, 2):
            tail_x(k).start()

    @pl.when(is_next)
    def _():
        to_other.start()

    seven = remote(lists.at[pl.ds(0, 7)], lists.at[pl.ds(0, 7)], ls, lr, other)
    seven.wait_recv()
    lane = lax.broadcasted_iota(jnp.int32, (1, 128), 1) // tiles
    picked = []
    for g in range(2):
        row = jnp.zeros((1, 128), F32)
        for d in range(4):
            row = jnp.where(lane == d, lists[g * 4 + d, tiles:tiles + 1, :], row)
        picked.append(row)
    ids = jnp.concatenate(picked, axis=1)
    target_row = (lax.broadcasted_iota(jnp.int32, (256, 256), 0) + x * 256).astype(F32)
    chosen = (target_row == ids).astype(F32).astype(BF16)
    rows = jnp.concatenate([lists[d, 0:tiles, :] for d in range(8)], axis=0)
    hi = rows.astype(BF16)
    rest = rows - hi.astype(F32)
    mid = rest.astype(BF16)
    low = (rest - mid.astype(F32)).astype(BF16)
    placed = jnp.dot(chosen, hi, preferred_element_type=F32)
    placed = placed + jnp.dot(chosen, mid, preferred_element_type=F32)
    placed = placed + jnp.dot(chosen, low, preferred_element_type=F32)
    p[...] = placed

    def chunk(k):
        return pl.ds(pl.multiple_of(k * 32, 32), 32)

    def all_of(buffer, send, recv):
        return remote(buffer, buffer, send, recv, other)

    for k in range(1, 8):
        remote(p.at[chunk((z + k) % 8)], sz.at[k - 1], rzs, rzr, z_peers[k - 1]).start()

    @pl.when(is_head)
    def _():
        to_other.wait_recv()
        for i in sent_blocks + (3, 7):
            block = head_block(i)
            out[i] = hg[block] + tin[block // 2, block % 2].T
            if i % 4 < 3:
                head_x(i, out.at[i]).start()

    @pl.when(is_next)
    def _():
        for i in (3, 7):
            out[i] = hg[head_block(i)]

    def x_total(c):
        acc = out[4 * c + 3]
        for k in range(3):
            head_x(4 * c + k, out.at[4 * c + k]).wait_recv()
            acc = acc + fin[c, k]
        return acc

    all_of(sz, rzs, rzr).wait_recv()
    acc = p[chunk(z), :]
    for k in range(7):
        acc = acc + sz[k]
    fz[0] = acc
    for k in range(1, 8):
        remote(fz.at[0], fz.at[k], bys, byr, y_peers[k - 1]).start()

    @pl.when(is_head)
    def _():
        for k in range(1, 4):
            tail_x(k).wait_recv()
        for c, parity in ((0, q_down), (1, 1 - q_down)):
            tsend[c] = tg[x, parity] + tfin[0, parity] + tfin[1, parity] + tfin[2, parity]
        tail_y(0, near_dev).start()
        tail_y(1, far_dev).start()


    all_of(fz.at[pl.ds(1, 7)], bys, byr).wait_recv()
    acc = fz[(y + 8) % 8]
    for i in range(1, 8):
        acc = acc + fz[(y - i + 8) % 8]
    slab = x * 256
    at_z = pl.ds(pl.multiple_of(slab + z * 32, 32), 32)
    full[at_z, :] = acc

    def third_z(k):
        return remote(full.at[at_z], full.at[at_z], azs.at[k - 1], azr.at[k - 1], z_peers[k - 1])

    def third_z_in(k):
        src = pl.ds(pl.multiple_of(slab + ((z - k + 8) % 8) * 32, 32), 32)
        return remote(full.at[src], full.at[src], azs.at[k - 1], azr.at[k - 1], z_peers[k - 1])

    for k in range(1, 8):
        third_z(k).start()

    ysend[...] = x_total(0)
    along_y = remote(ysend, yrecv, ps, pr, pair)
    along_y.start()

    def whole(xx):
        return pl.ds(pl.multiple_of(xx * 256, 256), 256)

    def spread(n):
        at = full.at[pl.ds(pl.multiple_of(slab + n * 32, 32), 32)]
        for k in (1, 3, 2):
            remote(at, at, gxs.at[k - 1], gxr.at[k - 1], x_peers[k - 1]).start()

    def gather_x_all(k):
        at = full.at[whole((x - k + 4) % 4)]
        return remote(at, at, gxs.at[k - 1], gxr.at[k - 1], x_peers[k - 1])

    def swap(k):
        at = whole((x - k + 4) % 4)
        return remote(full.at[at], peer.at[at], gcs.at[k], gcr.at[k], other)

    spread(z)
    for k in (1, 7, 2, 6, 3, 5, 4):
        third_z_in(k).wait_recv()
        spread((z - k + 8) % 8)
    swap(0).start()
    ent[...] = x_total(1)
    along_y.wait_recv()
    ent[...] += yrecv[...]

    @pl.when(is_next)
    def _():
        for c in range(2):
            tail_y(c, near_dev).wait_recv()
        ent[...] += (trecv[0] + trecv[1]).T

    for k in (1, 3, 2):
        gather_x_all(k).wait_recv()
        swap(k).start()

    n = rel.shape[0]

    @pl.when(is_head)
    def _():
        rel[:, 0:128] = full[0:n, :]

    @pl.when(is_next)
    def _():
        rel[:, 128:256] = full[0:n, :]

    for k in range(4):
        swap(k).wait_recv()

    @pl.when(is_head)
    def _():
        rel[:, 128:256] = peer[0:n, :]

    @pl.when(is_next)
    def _():
        rel[:, 0:128] = peer[0:n, :]

    seven.wait_send()
    for i in sent_blocks:
        head_x(i, out.at[i]).wait_send()

    @pl.when(is_head)
    def _():
        for k in range(1, 4):
            tail_x(k).wait_send()
        for c in range(2):
            tail_y(c, near_dev).wait_send()

    @pl.when(is_next)
    def _():
        to_other.wait_send()

    for k in range(1, 8):
        third_z(k).wait_send()
    all_of(sz, rzs, rzr).wait_send()
    all_of(fz.at[pl.ds(1, 7)], bys, byr).wait_send()
    along_y.wait_send()
    for k in range(1, 4):
        gather_x_all(k).wait_send()
    for k in range(4):
        swap(k).wait_send()


def reduce(hg, listed, xt, g_hi, g_lo, relations):
    whole = pl.BlockSpec(memory_space=VMEM)
    dma = pltpu.SemaphoreType.DMA
    rows = listed.shape[1]
    return pl.pallas_call(
        reduce_kernel,
        name="reduce_gradients",
        out_shape=(jax.ShapeDtypeStruct((BLOCK, WIDTH), F32), jax.ShapeDtypeStruct((relations, WIDTH), F32)),
        in_specs=[whole] * 5,
        out_specs=(whole, whole),
        scratch_shapes=[
            VMEM((4, 2, WIDTH, BLOCK), F32),
            VMEM((8, rows, 128), F32),
            VMEM((4, 2, WIDTH, BLOCK), F32),
            VMEM((BLOCKS, BLOCK, WIDTH), F32),
            VMEM((2, 3, BLOCK, WIDTH), F32),
            VMEM((3, 2, WIDTH, BLOCK), F32),
            VMEM((2, WIDTH, BLOCK), F32),
            VMEM((2, WIDTH, BLOCK), F32),
            VMEM((BLOCK, WIDTH), F32),
            VMEM((BLOCK, WIDTH), F32),
            VMEM((256, 128), F32),
            VMEM((7, 32, 128), F32),
            VMEM((8, 32, 128), F32),
            VMEM((REL_PAD, 128), F32),
            VMEM((REL_PAD, 128), F32),
            dma, dma,
            dma, dma,
            dma((8,)), dma((8,)),
            dma((3,)), dma((3,)),
            dma((2,)), dma((2,)),
            dma, dma,
            dma, dma, dma, dma,
            dma((7,)), dma((7,)),
            dma((3,)), dma((3,)),
            dma((4,)), dma((4,)),
        ],
        compiler_params=pltpu.CompilerParams(collective_id=1, has_side_effects=True, vmem_limit_bytes=24 << 20),
    )(hg, listed, xt, g_hi, g_lo)


def local(entity, rel_weight, tile_rel, tile_head, tile_tail, tile_mask, negatives, tile_count):
    ready = gather(entity, rel_weight, negatives, tile_mask, tile_rel, tile_head, tile_tail)
    hg, listed, xt, g_hi, g_lo = terms(*ready, tile_count)
    return reduce(hg, listed, xt, g_hi, g_lo, rel_weight.shape[0])


def solution(mesh):
    return jax.shard_map(
        local,
        mesh=mesh,
        in_specs=(
            P(("shard", "rep"), None),
            P(),
            P(("shard", "rep")),
            P(("shard", "rep")),
            P(("shard", "rep")),
            P(("shard", "rep"), None, None),
            P(("shard", "rep"), None),
            P(("shard", "rep")),
        ),
        out_specs=(P(("shard", "rep"), None), P()),
        check_vma=False,
    )
```

```python
import functools

import jax
import jax.numpy as jnp
from jax import lax
from jax.experimental import pallas as pl
from jax.experimental.pallas import tpu as pltpu
from jax.sharding import PartitionSpec as P

MESH = pl.DeviceIdType.MESH
VMEM = pltpu.VMEM
F32 = jnp.float32
BF16 = jnp.bfloat16
BLOCK = 128
WIDTH = 256
BLOCKS = 8
GROUP = 8
REL_PAD = 1024


def place():
    shard = lax.axis_index("shard")
    rep = lax.axis_index("rep")
    core = shard % 2
    y_lo = (shard // 2) % 4
    z = shard // 8
    x = rep // 2
    y = (rep % 2) * 4 + y_lo
    return x, y, z, core


def device(x, y, z, core):
    x = (x + 8) % 4
    y = (y + 16) % 8
    z = (z + 16) % 8
    return ((z * 4 + y % 4) * 2 + core, x * 2 + y // 4)


def greet(partners):
    barrier = pltpu.get_barrier_semaphore()
    for partner in partners:
        pl.semaphore_signal(barrier, inc=1, device_id=partner, device_id_type=MESH)
    pl.semaphore_wait(barrier, len(partners))


def remote(src, dst, send, recv, target):
    return pltpu.make_async_remote_copy(
        src_ref=src, dst_ref=dst, send_sem=send, recv_sem=recv, device_id=target, device_id_type=MESH
    )


def halves(value):
    hi = value.astype(BF16)
    lo = (value - hi.astype(F32)).astype(BF16)
    return hi, lo


def gather_kernel(
    own_ref, relw_in, negs_in, mask_in, rel_in, head_in, tail_in,
    head, t_cols, t_rows, relw, negs, mask, rel_s, head_s, tail_s,
    tail, ys, yr, xs, xr, cs, cr, ls, ms,
):
    x, y, z, core = place()
    brought = [(relw_in, relw), (negs_in, negs), (mask_in, mask), (rel_in, rel_s), (head_in, head_s), (tail_in, tail_s)]
    local_copies = [pltpu.make_async_copy(src, dst, ms.at[k]) for k, (src, dst) in enumerate(brought)]
    for c in local_copies:
        c.start()
    q = y // 4
    y_lo = y % 4
    pair = device(x, y + 4, z, core)
    other = device(x, y, z, 1 - core)
    x_peers = [device(x + k, y, z, core) for k in range(1, 4)]
    chain_dev = device(x, y + 2 * core - 1, z + core * (y_lo // 3) - (1 - core) * ((3 - y_lo) // 3), 1 - core)
    is_head = core == 0
    is_next = core == 1
    mine = 2 * x + q
    q_near = (q + (3 - y_lo) // 3) % 2
    half = BLOCK // 2
    keep = pltpu.make_async_copy(own_ref, head.at[mine], ls)
    keep.start()
    greet([pair, other, chain_dev] + x_peers)

    streams = [
        (head, q, 0, BLOCK),
        (tail, q_near, 0, BLOCK),
        (head, 1 - q, 0, half),
        (head, 1 - q, half, half),
        (tail, 1 - q_near, 0, half),
        (tail, 1 - q_near, half, half),
    ]

    def piece(i, xx):
        array, part, first, rows = streams[i]
        return array.at[2 * xx + part, pl.ds(first, rows)]

    def along_x(i, k):
        src = own_ref if i == 0 else piece(i, x)
        return remote(src, piece(i, x), xs.at[i, k - 1], xr.at[i, k - 1], x_peers[k - 1])

    def from_x(i, k):
        at = piece(i, (x - k + 4) % 4)
        return remote(at, at, xs.at[i, k - 1], xr.at[i, k - 1], x_peers[k - 1])

    def spread(i):
        for k in (1, 3, 2):
            along_x(i, k).start()

    def pair_copy(h):
        rows = pl.ds(h * half, half)
        return remote(own_ref.at[rows], head.at[mine, rows], ys.at[h], yr.at[h], pair)

    def pair_in(h):
        at = head.at[2 * x + 1 - q, pl.ds(h * half, half)]
        return remote(at, at, ys.at[h], yr.at[h], pair)

    near_copy = remote(own_ref, tail.at[mine], ys.at[2], yr.at[2], chain_dev)
    near_at = tail.at[2 * x + q_near]
    near_in = remote(near_at, near_at, ys.at[2], yr.at[2], chain_dev)

    def far_copy(h):
        at = (2 * x + 1 - q, pl.ds(h * half, half))
        return remote(head.at[at], tail.at[at], ys.at[3 + h], yr.at[3 + h], chain_dev)

    def far_in(h):
        at = tail.at[2 * x + 1 - q_near, pl.ds(h * half, half)]
        return remote(at, at, ys.at[3 + h], yr.at[3 + h], chain_dev)

    shared = [2 * ((x + k) % 4) + part for part in (q, 1 - q) for k in range(4)]

    def across(n):
        src = own_ref if n == 0 else head.at[shared[n]]
        return remote(src, tail.at[shared[n]], cs.at[n], cr.at[n], other)

    def across_in(n):
        return remote(tail.at[shared[n]], tail.at[shared[n]], cs.at[n], cr.at[n], other)

    def split(block):
        hi, lo = halves(tail[block])
        at = pl.ds(pl.multiple_of(block * BLOCK, BLOCK), BLOCK)
        t_cols[at, 0:256] = hi
        t_cols[at, 256:512] = hi
        t_cols[at, 512:768] = lo
        n, sub = block // 2, (block % 2) * BLOCK
        for k, part in enumerate((hi, hi, lo)):
            t_rows[n, pl.ds(pl.multiple_of(k * 256 + sub, BLOCK), BLOCK), :] = part

    @pl.when(is_next)
    def _():
        near_copy.start()

    pair_copy(0).start()
    pair_copy(1).start()
    spread(0)

    @pl.when(is_head)
    def _():
        across(0).start()
        near_in.wait_recv()
        spread(1)

    for h in range(2):
        pair_in(h).wait_recv()

        @pl.when(is_next)
        def _():
            far_copy(h).start()

        spread(2 + h)

    @pl.when(is_head)
    def _():
        across(4).start()
        far_in(0).wait_recv()
        spread(4)
        far_in(1).wait_recv()
        spread(5)

    for k in (3, 1, 2):
        from_x(0, (4 - k) % 4).wait_recv()

        @pl.when(is_head)
        def _():
            across(k).start()

    for k in (3, 1, 2):
        from_x(2, (4 - k) % 4).wait_recv()
        from_x(3, (4 - k) % 4).wait_recv()

        @pl.when(is_head)
        def _():
            across(4 + k).start()

    @pl.when(is_head)
    def _():
        split(2 * x + q_near)
        split(2 * x + 1 - q_near)
        for k in (1, 3, 2):
            from_x(1, k).wait_recv()
            split(2 * ((x - k + 4) % 4) + q_near)
        for k in (1, 3, 2):
            from_x(4, k).wait_recv()
            from_x(5, k).wait_recv()
            split(2 * ((x - k + 4) % 4) + 1 - q_near)

    @pl.when(is_next)
    def _():
        for n in range(8):
            across_in(n).wait_recv()
            split(shared[n])

    keep.wait()
    for c in local_copies:
        c.wait()
    for h in range(2):
        pair_copy(h).wait_send()
    for i in (0, 2, 3):
        for k in range(1, 4):
            along_x(i, k).wait_send()

    @pl.when(is_head)
    def _():
        for i in (1, 4, 5):
            for k in range(1, 4):
                along_x(i, k).wait_send()
        for n in range(8):
            across(n).wait_send()

    @pl.when(is_next)
    def _():
        near_copy.wait_send()
        far_copy(0).wait_send()
        far_copy(1).wait_send()


def gather(entity, rel_weight, negatives, tile_mask, tile_rel, tile_head, tile_tail):
    hbm = pl.BlockSpec(memory_space=pltpu.HBM)
    whole = pl.BlockSpec(memory_space=VMEM)
    scalars = pl.BlockSpec(memory_space=pltpu.SMEM)
    part = jax.ShapeDtypeStruct((BLOCKS, BLOCK, WIDTH), F32)
    operands = [entity, rel_weight, negatives, tile_mask, tile_rel, tile_head, tile_tail]
    operands = [pltpu.with_memory_space_constraint(a, pltpu.HBM) for a in operands]
    dma = pltpu.SemaphoreType.DMA
    return pl.pallas_call(
        gather_kernel,
        name="gather_partitions",
        out_shape=(
            part,
            jax.ShapeDtypeStruct((BLOCKS * BLOCK, 3 * WIDTH), BF16),
            jax.ShapeDtypeStruct((4, 3 * WIDTH, WIDTH), BF16),
            *[jax.ShapeDtypeStruct(a.shape, a.dtype) for a in operands[1:]],
        ),
        in_specs=[hbm] * 7,
        out_specs=(whole,) * 6 + (scalars,) * 3,
        scratch_shapes=[
            VMEM((BLOCKS, BLOCK, WIDTH), F32),
            dma((5,)), dma((5,)), dma((6, 3)), dma((6, 3)), dma((8,)), dma((8,)), dma, dma((6,)),
        ],
        compiler_params=pltpu.CompilerParams(collective_id=0, has_side_effects=True, vmem_limit_bytes=32 << 20),
    )(*operands)


def dot_nt(a, b):
    return lax.dot_general(a, b, (((1,), (1,)), ((), ())), preferred_element_type=F32)


def terms_kernel(
    rel_s, head_s, tail_s, count_s, head, t_cols, t_rows, relw, negs, mask, hgrad, tgrad, listed,
    xx, xt, scores, g_hi, g_lo, mixed, counts, edges,
):
    count = count_s[0]
    parts = 4
    rows = GROUP * BLOCK
    step = WIDTH
    tiles = mask.shape[0]

    hgrad[...] = jnp.zeros_like(hgrad)
    listed[...] = jnp.zeros_like(listed)
    tgrad[...] = jnp.zeros_like(tgrad)

    lane = lax.broadcasted_iota(jnp.int32, (8, 128), 1) % tiles
    ids = jnp.zeros((8, 128), F32)
    for tile in range(tiles):
        ids = jnp.where(lane == tile, rel_s[tile].astype(F32), ids)
    for c in range(2):
        listed[c, tiles:tiles + 8, :] = ids

    def do_group(group, carry):
        for j in range(GROUP):
            tile = group * GROUP + j
            at = pl.ds(j * BLOCK, BLOCK)
            scaled = head[head_s[tile]] * relw[pl.ds(rel_s[tile], 1), :]
            hi, lo = halves(scaled)
            xx[at, 0:256] = hi
            xx[at, 256:512] = lo
            xx[at, 512:768] = hi
            hi_t, lo_t = halves(scaled.T)
            xt[:, pl.ds(j * BLOCK, BLOCK)] = hi_t
            xt[:, pl.ds(rows + j * BLOCK, BLOCK)] = lo_t
            xt[:, pl.ds(2 * rows + j * BLOCK, BLOCK)] = hi_t
            live = (tile < count).astype(F32)
            drawn = negs[pl.ds(tile, 1), :]
            upper = (lax.broadcasted_iota(jnp.int32, (BLOCKS, 256), 0) == drawn // BLOCK).astype(F32)
            lower = (lax.broadcasted_iota(jnp.int32, (BLOCK, 256), 0) == drawn % BLOCK).astype(F32)
            counts[j] = dot_nt(upper.astype(BF16), lower.astype(BF16)) * live

        def make_scores(n):
            scores[n] = dot_nt(xx[...], t_cols[pl.ds(n * step, step), :])

        def make_edges(j):
            tile = group * GROUP + j
            b = tail_s[tile]
            at = pl.ds(pl.multiple_of((b % 2) * BLOCK, BLOCK), BLOCK)
            own = scores[b // 2, pl.ds(j * BLOCK, BLOCK), at]
            live = jnp.where(tile < count, 1.0, 0.0).astype(F32)
            edges[j] = (mask[tile].astype(F32) * live) * lax.logistic(-own)

        def make_grads(n):
            for j in range(GROUP):
                tile = group * GROUP + j
                at = pl.ds(j * BLOCK, BLOCK)
                for h in range(2):
                    b = 2 * n + h
                    lanes = slice(h * BLOCK, (h + 1) * BLOCK)
                    here = jnp.where(tail_s[tile] == b, 1.0, 0.0).astype(F32)
                    g = counts[j, b:b + 1, :] * lax.logistic(scores[n, at, lanes]) - here * edges[j]
                    hi, lo = halves(g)
                    g_hi[n, at, lanes] = hi
                    g_lo[n, at, lanes] = lo

        def make_tail(n):
            weights = jnp.concatenate([g_hi[n], g_hi[n], g_lo[n]], axis=0)
            part = jnp.dot(xt[...], weights, preferred_element_type=F32)
            tgrad[n, 0] += part[:, 0:BLOCK]
            tgrad[n, 1] += part[:, BLOCK:]

        def make_mixed(n):
            rows_in = jnp.concatenate([g_hi[n], g_lo[n], g_hi[n]], axis=1)
            part = jnp.dot(rows_in, t_rows[n], preferred_element_type=F32)
            if n == 0:
                mixed[...] = part
            else:
                mixed[...] += part

        for n in range(parts):
            make_scores(n)
        for j in range(GROUP):
            make_edges(j)
        for n in range(parts):
            make_grads(n)
            make_mixed(n)
            make_tail(n)

        for j in range(GROUP):
            tile = group * GROUP + j
            at = pl.ds(j * BLOCK, BLOCK)
            h, r = head_s[tile], rel_s[tile]
            m = mixed[at, :]
            hgrad[h] += m * relw[pl.ds(r, 1), :]
            row = jnp.sum(head[h] * m, axis=0, keepdims=True)
            listed[0, pl.ds(tile, 1), :] = row[:, 0:128]
            listed[1, pl.ds(tile, 1), :] = row[:, 128:256]
        return carry

    lax.fori_loop(0, (count + GROUP - 1) // GROUP, do_group, 0)


def terms(head, t_cols, t_rows, relw, negs, mask, rel_s, head_s, tail_s, count_s):
    rows = GROUP * BLOCK
    tiles = mask.shape[0]
    whole = pl.BlockSpec(memory_space=VMEM)
    scalars = pl.BlockSpec(memory_space=pltpu.SMEM)
    part = jax.ShapeDtypeStruct((BLOCKS, BLOCK, WIDTH), F32)
    return pl.pallas_call(
        terms_kernel,
        name="tile_terms",
        out_shape=(part, jax.ShapeDtypeStruct((4, 2, WIDTH, BLOCK), F32), jax.ShapeDtypeStruct((2, tiles + 8, 128), F32)),
        in_specs=[scalars] * 4 + [whole] * 6,
        out_specs=(whole, whole, whole),
        scratch_shapes=[
            VMEM((rows, 3 * WIDTH), BF16),
            VMEM((WIDTH, 3 * rows), BF16),
            VMEM((4, rows, WIDTH), F32),
            VMEM((4, rows, WIDTH), BF16),
            VMEM((4, rows, WIDTH), BF16),
            VMEM((rows, WIDTH), F32),
            VMEM((GROUP, BLOCKS, BLOCK), F32),
            VMEM((GROUP, BLOCK, BLOCK), F32),
        ],
        compiler_params=pltpu.CompilerParams(vmem_limit_bytes=40 << 20),
    )(rel_s, head_s, tail_s, count_s, head, t_cols, t_rows, relw, negs, mask)


def reduce_kernel(
    hg, tg, listed, ent, rel,
    lists, tin, out, fin, tfin, tsend, trecv, ysend, yrecv, p, sz, fz, full, peer,
    ls, lr, ts, tr, xs, xr, us, ur, vs, vr, ps, pr, rzs, rzr, bys, byr, azs, azr, gxs, gxr, gcs, gcr,
):
    x, y, z, core = place()
    q = y // 4
    pair = device(x, y + 4, z, core)
    other = device(x, y, z, 1 - core)
    x_peers = [device(x + k, y, z, core) for k in range(1, 4)]
    x_over = [device(x + k, y, z, 1 - core) for k in range(1, 4)]
    y_peers = [device(x, y + k, z, core) for k in range(1, 8)]
    z_peers = [device(x, y, z + k, core) for k in range(1, 8)]
    y_lo = y % 4
    sign = 2 * core - 1
    z_there = z + core * (y_lo // 3) - (1 - core) * ((3 - y_lo) // 3)
    near_dev = device(x, y + sign, z_there, 1 - core)
    far_dev = device(x, y + 5 * sign, z_there, 1 - core)
    is_head = core == 0
    is_next = core == 1
    greet(x_peers + x_over + y_peers + z_peers + [other, near_dev, far_dev])
    me = core * 4 + x
    tiles = listed.shape[1] - 8

    targets = [(x_peers[k - 1], core, k - 1) for k in range(1, 4)]
    targets += [(x_over[k - 1], 1 - core, 2 + k) for k in range(1, 4)]
    targets += [(other, 1 - core, 6)]

    def list_copy(i):
        target, columns, k = targets[i]
        return remote(listed.at[columns], lists.at[me], ls, lr, target)

    for i in range(7):
        list_copy(i).start()
    lists[me] = listed[core]

    to_other = remote(tg, tin, ts, tr, other)
    q_down = ((y + 7) % 8) // 4

    def tail_x(k):
        return remote(tg.at[(x + k) % 4], tfin.at[k - 1], us.at[k - 1], ur.at[k - 1], x_peers[k - 1])

    def head_block(i):
        return 2 * ((x + 1 + i % 4) % 4) + (1 - q if i < 4 else q)

    def head_x(i, src):
        k = i % 4 + 1
        return remote(src, fin.at[i // 4, k - 1], xs.at[i], xr.at[i], x_peers[k - 1])

    def tail_y(c, target):
        return remote(tsend.at[c], trecv.at[c], vs.at[c], vr.at[c], target)

    sent_blocks = (0, 2, 1, 4, 6, 5)

    @pl.when(is_head)
    def _():
        for k in (1, 3, 2):
            tail_x(k).start()

    @pl.when(is_next)
    def _():
        to_other.start()
        for i in sent_blocks:
            head_x(i, hg.at[head_block(i)]).start()

    seven = remote(lists.at[pl.ds(0, 7)], lists.at[pl.ds(0, 7)], ls, lr, other)
    seven.wait_recv()
    lane = lax.broadcasted_iota(jnp.int32, (1, 128), 1) // tiles
    picked = []
    for g in range(2):
        row = jnp.zeros((1, 128), F32)
        for d in range(4):
            row = jnp.where(lane == d, lists[g * 4 + d, tiles:tiles + 1, :], row)
        picked.append(row)
    ids = jnp.concatenate(picked, axis=1)
    target_row = (lax.broadcasted_iota(jnp.int32, (256, 256), 0) + x * 256).astype(F32)
    chosen = (target_row == ids).astype(F32).astype(BF16)
    rows = jnp.concatenate([lists[d, 0:tiles, :] for d in range(8)], axis=0)
    hi = rows.astype(BF16)
    rest = rows - hi.astype(F32)
    mid = rest.astype(BF16)
    low = (rest - mid.astype(F32)).astype(BF16)
    placed = jnp.dot(chosen, hi, preferred_element_type=F32)
    placed = placed + jnp.dot(chosen, mid, preferred_element_type=F32)
    placed = placed + jnp.dot(chosen, low, preferred_element_type=F32)
    p[...] = placed

    def chunk(k):
        return pl.ds(pl.multiple_of(k * 32, 32), 32)

    def all_of(buffer, send, recv):
        return remote(buffer, buffer, send, recv, other)

    for k in range(1, 8):
        remote(p.at[chunk((z + k) % 8)], sz.at[k - 1], rzs, rzr, z_peers[k - 1]).start()

    @pl.when(is_head)
    def _():
        to_other.wait_recv()
        for i in sent_blocks + (3, 7):
            block = head_block(i)
            out[i] = hg[block] + tin[block // 2, block % 2].T
            if i % 4 < 3:
                head_x(i, out.at[i]).start()

    @pl.when(is_next)
    def _():
        for i in (3, 7):
            out[i] = hg[head_block(i)]

    def x_total(c):
        acc = out[4 * c + 3]
        for k in range(3):
            head_x(4 * c + k, out.at[4 * c + k]).wait_recv()
            acc = acc + fin[c, k]
        return acc

    all_of(sz, rzs, rzr).wait_recv()
    acc = p[chunk(z), :]
    for k in range(7):
        acc = acc + sz[k]
    fz[0] = acc
    for k in range(1, 8):
        remote(fz.at[0], fz.at[k], bys, byr, y_peers[k - 1]).start()

    @pl.when(is_head)
    def _():
        for k in range(1, 4):
            tail_x(k).wait_recv()
        for c, parity in ((0, q_down), (1, 1 - q_down)):
            tsend[c] = tg[x, parity] + tfin[0, parity] + tfin[1, parity] + tfin[2, parity]
        tail_y(0, near_dev).start()
        tail_y(1, far_dev).start()


    all_of(fz.at[pl.ds(1, 7)], bys, byr).wait_recv()
    acc = fz[(y + 8) % 8]
    for i in range(1, 8):
        acc = acc + fz[(y - i + 8) % 8]
    slab = x * 256
    at_z = pl.ds(pl.multiple_of(slab + z * 32, 32), 32)
    full[at_z, :] = acc

    def third_z(k):
        return remote(full.at[at_z], full.at[at_z], azs.at[k - 1], azr.at[k - 1], z_peers[k - 1])

    def third_z_in(k):
        src = pl.ds(pl.multiple_of(slab + ((z - k + 8) % 8) * 32, 32), 32)
        return remote(full.at[src], full.at[src], azs.at[k - 1], azr.at[k - 1], z_peers[k - 1])

    for k in range(1, 8):
        third_z(k).start()

    ysend[...] = x_total(0)
    along_y = remote(ysend, yrecv, ps, pr, pair)
    along_y.start()

    def whole(xx):
        return pl.ds(pl.multiple_of(xx * 256, 256), 256)

    def spread(n):
        at = full.at[pl.ds(pl.multiple_of(slab + n * 32, 32), 32)]
        for k in (1, 3, 2):
            remote(at, at, gxs.at[k - 1], gxr.at[k - 1], x_peers[k - 1]).start()

    def gather_x_all(k):
        at = full.at[whole((x - k + 4) % 4)]
        return remote(at, at, gxs.at[k - 1], gxr.at[k - 1], x_peers[k - 1])

    def swap(k):
        at = whole((x - k + 4) % 4)
        return remote(full.at[at], peer.at[at], gcs.at[k], gcr.at[k], other)

    spread(z)
    for k in (1, 7, 2, 6, 3, 5, 4):
        third_z_in(k).wait_recv()
        spread((z - k + 8) % 8)
    swap(0).start()
    ent[...] = x_total(1)
    along_y.wait_recv()
    ent[...] += yrecv[...]

    @pl.when(is_next)
    def _():
        for c in range(2):
            tail_y(c, near_dev).wait_recv()
        ent[...] += (trecv[0] + trecv[1]).T

    for k in (1, 3, 2):
        gather_x_all(k).wait_recv()
        swap(k).start()

    n = rel.shape[0]

    @pl.when(is_head)
    def _():
        rel[:, 0:128] = full[0:n, :]

    @pl.when(is_next)
    def _():
        rel[:, 128:256] = full[0:n, :]

    for k in range(4):
        swap(k).wait_recv()

    @pl.when(is_head)
    def _():
        rel[:, 128:256] = peer[0:n, :]

    @pl.when(is_next)
    def _():
        rel[:, 0:128] = peer[0:n, :]

    seven.wait_send()
    for i in sent_blocks:
        head_x(i, out.at[i]).wait_send()

    @pl.when(is_head)
    def _():
        for k in range(1, 4):
            tail_x(k).wait_send()
        for c in range(2):
            tail_y(c, near_dev).wait_send()

    @pl.when(is_next)
    def _():
        to_other.wait_send()

    for k in range(1, 8):
        third_z(k).wait_send()
    all_of(sz, rzs, rzr).wait_send()
    all_of(fz.at[pl.ds(1, 7)], bys, byr).wait_send()
    along_y.wait_send()
    for k in range(1, 4):
        gather_x_all(k).wait_send()
    for k in range(4):
        swap(k).wait_send()


def reduce(hg, tg, listed, relations):
    whole = pl.BlockSpec(memory_space=VMEM)
    dma = pltpu.SemaphoreType.DMA
    rows = listed.shape[1]
    return pl.pallas_call(
        reduce_kernel,
        name="reduce_gradients",
        out_shape=(jax.ShapeDtypeStruct((BLOCK, WIDTH), F32), jax.ShapeDtypeStruct((relations, WIDTH), F32)),
        in_specs=[whole] * 3,
        out_specs=(whole, whole),
        scratch_shapes=[
            VMEM((8, rows, 128), F32),
            VMEM((4, 2, WIDTH, BLOCK), F32),
            VMEM((BLOCKS, BLOCK, WIDTH), F32),
            VMEM((2, 3, BLOCK, WIDTH), F32),
            VMEM((3, 2, WIDTH, BLOCK), F32),
            VMEM((2, WIDTH, BLOCK), F32),
            VMEM((2, WIDTH, BLOCK), F32),
            VMEM((BLOCK, WIDTH), F32),
            VMEM((BLOCK, WIDTH), F32),
            VMEM((256, 128), F32),
            VMEM((7, 32, 128), F32),
            VMEM((8, 32, 128), F32),
            VMEM((REL_PAD, 128), F32),
            VMEM((REL_PAD, 128), F32),
            dma, dma,
            dma, dma,
            dma((8,)), dma((8,)),
            dma((3,)), dma((3,)),
            dma((2,)), dma((2,)),
            dma, dma,
            dma, dma, dma, dma,
            dma((7,)), dma((7,)),
            dma((3,)), dma((3,)),
            dma((4,)), dma((4,)),
        ],
        compiler_params=pltpu.CompilerParams(collective_id=1, has_side_effects=True, vmem_limit_bytes=40 << 20),
    )(hg, tg, listed)


def local(entity, rel_weight, tile_rel, tile_head, tile_tail, tile_mask, negatives, tile_count):
    ready = gather(entity, rel_weight, negatives, tile_mask, tile_rel, tile_head, tile_tail)
    hg, tg, listed = terms(*ready, tile_count)
    return reduce(hg, tg, listed, rel_weight.shape[0])


def solution(mesh):
    return jax.shard_map(
        local,
        mesh=mesh,
        in_specs=(
            P(("shard", "rep"), None),
            P(),
            P(("shard", "rep")),
            P(("shard", "rep")),
            P(("shard", "rep")),
            P(("shard", "rep"), None, None),
            P(("shard", "rep"), None),
            P(("shard", "rep")),
        ),
        out_specs=(P(("shard", "rep"), None), P()),
        check_vma=False,
    )
```

```python
import functools

import jax
import jax.numpy as jnp
from jax import lax
from jax.experimental import pallas as pl
from jax.experimental.pallas import tpu as pltpu
from jax.sharding import PartitionSpec as P

MESH = pl.DeviceIdType.MESH
VMEM = pltpu.VMEM
F32 = jnp.float32
BF16 = jnp.bfloat16
BLOCK = 128
WIDTH = 256
BLOCKS = 8
GROUP = 8
REL_PAD = 1024


def place():
    shard = lax.axis_index("shard")
    rep = lax.axis_index("rep")
    core = shard % 2
    y_lo = (shard // 2) % 4
    z = shard // 8
    x = rep // 2
    y = (rep % 2) * 4 + y_lo
    return x, y, z, core


def device(x, y, z, core):
    x = (x + 8) % 4
    y = (y + 16) % 8
    z = (z + 16) % 8
    return ((z * 4 + y % 4) * 2 + core, x * 2 + y // 4)


def greet(partners):
    barrier = pltpu.get_barrier_semaphore()
    for partner in partners:
        pl.semaphore_signal(barrier, inc=1, device_id=partner, device_id_type=MESH)
    pl.semaphore_wait(barrier, len(partners))


def remote(src, dst, send, recv, target):
    return pltpu.make_async_remote_copy(
        src_ref=src, dst_ref=dst, send_sem=send, recv_sem=recv, device_id=target, device_id_type=MESH
    )


def halves(value):
    hi = value.astype(BF16)
    lo = (value - hi.astype(F32)).astype(BF16)
    return hi, lo


def gather_kernel(
    own_ref, relw_in, negs_in, mask_in, rel_in, head_in, tail_in,
    head, t_cols, t_rows, relw, negs, mask, rel_s, head_s, tail_s,
    tail, ys, yr, xs, xr, cs, cr, ls, ms,
):
    x, y, z, core = place()
    brought = [(relw_in, relw), (negs_in, negs), (mask_in, mask), (rel_in, rel_s), (head_in, head_s), (tail_in, tail_s)]
    local_copies = [pltpu.make_async_copy(src, dst, ms.at[k]) for k, (src, dst) in enumerate(brought)]
    for c in local_copies:
        c.start()
    q = y // 4
    y_lo = y % 4
    pair = device(x, y + 4, z, core)
    other = device(x, y, z, 1 - core)
    x_peers = [device(x + k, y, z, core) for k in range(1, 4)]
    chain_dev = device(x, y + 2 * core - 1, z + core * (y_lo // 3) - (1 - core) * ((3 - y_lo) // 3), 1 - core)
    is_head = core == 0
    is_next = core == 1
    mine = 2 * x + q
    q_near = (q + (3 - y_lo) // 3) % 2
    half = BLOCK // 2
    keep = pltpu.make_async_copy(own_ref, head.at[mine], ls)
    keep.start()
    greet([pair, other, chain_dev] + x_peers)

    streams = [
        (head, q, 0, BLOCK),
        (tail, q_near, 0, BLOCK),
        (head, 1 - q, 0, half),
        (head, 1 - q, half, half),
        (tail, 1 - q_near, 0, half),
        (tail, 1 - q_near, half, half),
    ]

    def piece(i, xx):
        array, part, first, rows = streams[i]
        return array.at[2 * xx + part, pl.ds(first, rows)]

    def along_x(i, k):
        src = own_ref if i == 0 else piece(i, x)
        return remote(src, piece(i, x), xs.at[i, k - 1], xr.at[i, k - 1], x_peers[k - 1])

    def from_x(i, k):
        at = piece(i, (x - k + 4) % 4)
        return remote(at, at, xs.at[i, k - 1], xr.at[i, k - 1], x_peers[k - 1])

    def spread(i):
        for k in (1, 3, 2):
            along_x(i, k).start()

    def pair_copy(h):
        rows = pl.ds(h * half, half)
        return remote(own_ref.at[rows], head.at[mine, rows], ys.at[h], yr.at[h], pair)

    def pair_in(h):
        at = head.at[2 * x + 1 - q, pl.ds(h * half, half)]
        return remote(at, at, ys.at[h], yr.at[h], pair)

    near_copy = remote(own_ref, tail.at[mine], ys.at[2], yr.at[2], chain_dev)
    near_at = tail.at[2 * x + q_near]
    near_in = remote(near_at, near_at, ys.at[2], yr.at[2], chain_dev)

    def far_copy(h):
        at = (2 * x + 1 - q, pl.ds(h * half, half))
        return remote(head.at[at], tail.at[at], ys.at[3 + h], yr.at[3 + h], chain_dev)

    def far_in(h):
        at = tail.at[2 * x + 1 - q_near, pl.ds(h * half, half)]
        return remote(at, at, ys.at[3 + h], yr.at[3 + h], chain_dev)

    shared = [2 * ((x + k) % 4) + part for part in (q, 1 - q) for k in range(4)]

    def across(n):
        src = own_ref if n == 0 else head.at[shared[n]]
        return remote(src, tail.at[shared[n]], cs.at[n], cr.at[n], other)

    def across_in(n):
        return remote(tail.at[shared[n]], tail.at[shared[n]], cs.at[n], cr.at[n], other)

    def split(block):
        hi, lo = halves(tail[block])
        at = pl.ds(pl.multiple_of(block * BLOCK, BLOCK), BLOCK)
        t_cols[at, 0:256] = hi
        t_cols[at, 256:512] = hi
        t_cols[at, 512:768] = lo
        n, sub = block // 2, (block % 2) * BLOCK
        for k, part in enumerate((hi, hi, lo)):
            t_rows[n, pl.ds(pl.multiple_of(k * 256 + sub, BLOCK), BLOCK), :] = part

    @pl.when(is_next)
    def _():
        near_copy.start()

    pair_copy(0).start()
    pair_copy(1).start()
    spread(0)

    @pl.when(is_head)
    def _():
        across(0).start()
        near_in.wait_recv()
        spread(1)

    for h in range(2):
        pair_in(h).wait_recv()

        @pl.when(is_next)
        def _():
            far_copy(h).start()

        spread(2 + h)

    @pl.when(is_head)
    def _():
        across(4).start()
        far_in(0).wait_recv()
        spread(4)
        far_in(1).wait_recv()
        spread(5)

    for k in (3, 1, 2):
        from_x(0, (4 - k) % 4).wait_recv()

        @pl.when(is_head)
        def _():
            across(k).start()

    for k in (3, 1, 2):
        from_x(2, (4 - k) % 4).wait_recv()
        from_x(3, (4 - k) % 4).wait_recv()

        @pl.when(is_head)
        def _():
            across(4 + k).start()

    @pl.when(is_head)
    def _():
        split(2 * x + q_near)
        split(2 * x + 1 - q_near)
        for k in (1, 3, 2):
            from_x(1, k).wait_recv()
            split(2 * ((x - k + 4) % 4) + q_near)
        for k in (1, 3, 2):
            from_x(4, k).wait_recv()
            from_x(5, k).wait_recv()
            split(2 * ((x - k + 4) % 4) + 1 - q_near)

    @pl.when(is_next)
    def _():
        for n in range(8):
            across_in(n).wait_recv()
            split(shared[n])

    keep.wait()
    for c in local_copies:
        c.wait()
    for h in range(2):
        pair_copy(h).wait_send()
    for i in (0, 2, 3):
        for k in range(1, 4):
            along_x(i, k).wait_send()

    @pl.when(is_head)
    def _():
        for i in (1, 4, 5):
            for k in range(1, 4):
                along_x(i, k).wait_send()
        for n in range(8):
            across(n).wait_send()

    @pl.when(is_next)
    def _():
        near_copy.wait_send()
        far_copy(0).wait_send()
        far_copy(1).wait_send()


def gather(entity, rel_weight, negatives, tile_mask, tile_rel, tile_head, tile_tail):
    hbm = pl.BlockSpec(memory_space=pltpu.HBM)
    whole = pl.BlockSpec(memory_space=VMEM)
    scalars = pl.BlockSpec(memory_space=pltpu.SMEM)
    part = jax.ShapeDtypeStruct((BLOCKS, BLOCK, WIDTH), F32)
    operands = [entity, rel_weight, negatives, tile_mask, tile_rel, tile_head, tile_tail]
    operands = [pltpu.with_memory_space_constraint(a, pltpu.HBM) for a in operands]
    dma = pltpu.SemaphoreType.DMA
    return pl.pallas_call(
        gather_kernel,
        name="gather_partitions",
        out_shape=(
            part,
            jax.ShapeDtypeStruct((BLOCKS * BLOCK, 3 * WIDTH), BF16),
            jax.ShapeDtypeStruct((4, 3 * WIDTH, WIDTH), BF16),
            *[jax.ShapeDtypeStruct(a.shape, a.dtype) for a in operands[1:]],
        ),
        in_specs=[hbm] * 7,
        out_specs=(whole,) * 6 + (scalars,) * 3,
        scratch_shapes=[
            VMEM((BLOCKS, BLOCK, WIDTH), F32),
            dma((5,)), dma((5,)), dma((6, 3)), dma((6, 3)), dma((8,)), dma((8,)), dma, dma((6,)),
        ],
        compiler_params=pltpu.CompilerParams(collective_id=0, has_side_effects=True, vmem_limit_bytes=32 << 20),
    )(*operands)


def dot_nt(a, b):
    return lax.dot_general(a, b, (((1,), (1,)), ((), ())), preferred_element_type=F32)


def terms_kernel(
    rel_s, head_s, tail_s, count_s, head, t_cols, t_rows, relw, negs, mask, hgrad, tgrad, listed,
    xx, xt, scores, g_hi, g_lo, mixed, counts, edges,
):
    count = count_s[0]
    parts = 4
    rows = GROUP * BLOCK
    step = WIDTH
    tiles = mask.shape[0]

    hgrad[...] = jnp.zeros_like(hgrad)
    listed[...] = jnp.zeros_like(listed)
    tgrad[...] = jnp.zeros_like(tgrad)

    lane = lax.broadcasted_iota(jnp.int32, (8, 128), 1) % tiles
    ids = jnp.zeros((8, 128), F32)
    for tile in range(tiles):
        ids = jnp.where(lane == tile, rel_s[tile].astype(F32), ids)
    for c in range(2):
        listed[c, tiles:tiles + 8, :] = ids

    def do_group(group, carry):
        for j in range(GROUP):
            tile = group * GROUP + j
            at = pl.ds(j * BLOCK, BLOCK)
            scaled = head[head_s[tile]] * relw[pl.ds(rel_s[tile], 1), :]
            hi, lo = halves(scaled)
            xx[at, 0:256] = hi
            xx[at, 256:512] = lo
            xx[at, 512:768] = hi
            hi_t, lo_t = halves(scaled.T)
            xt[:, pl.ds(j * BLOCK, BLOCK)] = hi_t
            xt[:, pl.ds(rows + j * BLOCK, BLOCK)] = lo_t
            xt[:, pl.ds(2 * rows + j * BLOCK, BLOCK)] = hi_t
            live = (tile < count).astype(F32)
            drawn = negs[pl.ds(tile, 1), :]
            upper = (lax.broadcasted_iota(jnp.int32, (BLOCKS, 256), 0) == drawn // BLOCK).astype(F32)
            lower = (lax.broadcasted_iota(jnp.int32, (BLOCK, 256), 0) == drawn % BLOCK).astype(F32)
            counts[j] = dot_nt(upper.astype(BF16), lower.astype(BF16)) * live

        def make_scores(n):
            scores[n] = dot_nt(xx[...], t_cols[pl.ds(n * step, step), :])

        def make_edges(j):
            tile = group * GROUP + j
            b = tail_s[tile]
            at = pl.ds(pl.multiple_of((b % 2) * BLOCK, BLOCK), BLOCK)
            own = scores[b // 2, pl.ds(j * BLOCK, BLOCK), at]
            live = jnp.where(tile < count, 1.0, 0.0).astype(F32)
            edges[j] = (mask[tile].astype(F32) * live) * lax.logistic(-own)

        def make_grads(n):
            for j in range(GROUP):
                tile = group * GROUP + j
                at = pl.ds(j * BLOCK, BLOCK)
                for h in range(2):
                    b = 2 * n + h
                    lanes = slice(h * BLOCK, (h + 1) * BLOCK)
                    here = jnp.where(tail_s[tile] == b, 1.0, 0.0).astype(F32)
                    g = counts[j, b:b + 1, :] * lax.logistic(scores[n, at, lanes]) - here * edges[j]
                    hi, lo = halves(g)
                    g_hi[n, at, lanes] = hi
                    g_lo[n, at, lanes] = lo

        def make_tail(n):
            weights = jnp.concatenate([g_hi[n], g_hi[n], g_lo[n]], axis=0)
            part = jnp.dot(xt[...], weights, preferred_element_type=F32)
            tgrad[n, 0] += part[:, 0:BLOCK]
            tgrad[n, 1] += part[:, BLOCK:]

        def make_mixed(n):
            rows_in = jnp.concatenate([g_hi[n], g_lo[n], g_hi[n]], axis=1)
            part = jnp.dot(rows_in, t_rows[n], preferred_element_type=F32)
            if n == 0:
                mixed[...] = part
            else:
                mixed[...] += part

        for n in range(parts):
            make_scores(n)
        for j in range(GROUP):
            make_edges(j)
        for n in range(parts):
            make_grads(n)
            make_mixed(n)
            make_tail(n)

        for j in range(GROUP):
            tile = group * GROUP + j
            at = pl.ds(j * BLOCK, BLOCK)
            h, r = head_s[tile], rel_s[tile]
            m = mixed[at, :]
            hgrad[h] += m * relw[pl.ds(r, 1), :]
            row = jnp.sum(head[h] * m, axis=0, keepdims=True)
            listed[0, pl.ds(tile, 1), :] = row[:, 0:128]
            listed[1, pl.ds(tile, 1), :] = row[:, 128:256]
        return carry

    lax.fori_loop(0, (count + GROUP - 1) // GROUP, do_group, 0)


def terms(head, t_cols, t_rows, relw, negs, mask, rel_s, head_s, tail_s, count_s):
    rows = GROUP * BLOCK
    tiles = mask.shape[0]
    whole = pl.BlockSpec(memory_space=VMEM)
    scalars = pl.BlockSpec(memory_space=pltpu.SMEM)
    part = jax.ShapeDtypeStruct((BLOCKS, BLOCK, WIDTH), F32)
    return pl.pallas_call(
        terms_kernel,
        name="tile_terms",
        out_shape=(part, jax.ShapeDtypeStruct((4, 2, WIDTH, BLOCK), F32), jax.ShapeDtypeStruct((2, tiles + 8, 128), F32)),
        in_specs=[scalars] * 4 + [whole] * 6,
        out_specs=(whole, whole, whole),
        scratch_shapes=[
            VMEM((rows, 3 * WIDTH), BF16),
            VMEM((WIDTH, 3 * rows), BF16),
            VMEM((4, rows, WIDTH), F32),
            VMEM((4, rows, WIDTH), BF16),
            VMEM((4, rows, WIDTH), BF16),
            VMEM((rows, WIDTH), F32),
            VMEM((GROUP, BLOCKS, BLOCK), F32),
            VMEM((GROUP, BLOCK, BLOCK), F32),
        ],
        compiler_params=pltpu.CompilerParams(vmem_limit_bytes=40 << 20),
    )(rel_s, head_s, tail_s, count_s, head, t_cols, t_rows, relw, negs, mask)


def reduce_kernel(
    hg, tg, listed, ent, rel,
    lists, tin, out, fin, tfin, tsend, trecv, ysend, yrecv, p, sz, fz, full, peer,
    ls, lr, ts, tr, xs, xr, us, ur, vs, vr, ps, pr, rzs, rzr, bys, byr, azs, azr, gxs, gxr, gcs, gcr,
):
    x, y, z, core = place()
    q = y // 4
    pair = device(x, y + 4, z, core)
    other = device(x, y, z, 1 - core)
    x_peers = [device(x + k, y, z, core) for k in range(1, 4)]
    x_over = [device(x + k, y, z, 1 - core) for k in range(1, 4)]
    y_peers = [device(x, y + k, z, core) for k in range(1, 8)]
    z_peers = [device(x, y, z + k, core) for k in range(1, 8)]
    y_lo = y % 4
    sign = 2 * core - 1
    z_there = z + core * (y_lo // 3) - (1 - core) * ((3 - y_lo) // 3)
    near_dev = device(x, y + sign, z_there, 1 - core)
    far_dev = device(x, y + 5 * sign, z_there, 1 - core)
    is_head = core == 0
    is_next = core == 1
    greet(x_peers + x_over + y_peers + z_peers + [other, near_dev, far_dev])
    me = core * 4 + x
    tiles = listed.shape[1] - 8

    targets = [(x_peers[k - 1], core, k - 1) for k in range(1, 4)]
    targets += [(x_over[k - 1], 1 - core, 2 + k) for k in range(1, 4)]
    targets += [(other, 1 - core, 6)]

    def list_copy(i):
        target, columns, k = targets[i]
        return remote(listed.at[columns], lists.at[me], ls, lr, target)

    for i in range(7):
        list_copy(i).start()
    lists[me] = listed[core]

    to_other = remote(tg, tin, ts, tr, other)
    q_down = ((y + 7) % 8) // 4

    def tail_x(k):
        return remote(tg.at[(x + k) % 4], tfin.at[k - 1], us.at[k - 1], ur.at[k - 1], x_peers[k - 1])

    def head_block(i):
        return 2 * ((x + 1 + i % 4) % 4) + (1 - q if i < 4 else q)

    def head_x(i, src):
        k = i % 4 + 1
        return remote(src, fin.at[i // 4, k - 1], xs.at[i], xr.at[i], x_peers[k - 1])

    def tail_y(c, target):
        return remote(tsend.at[c], trecv.at[c], vs.at[c], vr.at[c], target)

    sent_blocks = (0, 2, 1, 4, 6, 5)

    @pl.when(is_head)
    def _():
        for k in (1, 3, 2):
            tail_x(k).start()

    @pl.when(is_next)
    def _():
        to_other.start()
        for i in sent_blocks:
            head_x(i, hg.at[head_block(i)]).start()

    seven = remote(lists.at[pl.ds(0, 7)], lists.at[pl.ds(0, 7)], ls, lr, other)
    seven.wait_recv()
    lane = lax.broadcasted_iota(jnp.int32, (1, 128), 1) // tiles
    picked = []
    for g in range(2):
        row = jnp.zeros((1, 128), F32)
        for d in range(4):
            row = jnp.where(lane == d, lists[g * 4 + d, tiles:tiles + 1, :], row)
        picked.append(row)
    ids = jnp.concatenate(picked, axis=1)
    target_row = (lax.broadcasted_iota(jnp.int32, (256, 256), 0) + x * 256).astype(F32)
    chosen = (target_row == ids).astype(F32).astype(BF16)
    rows = jnp.concatenate([lists[d, 0:tiles, :] for d in range(8)], axis=0)
    hi = rows.astype(BF16)
    rest = rows - hi.astype(F32)
    mid = rest.astype(BF16)
    low = (rest - mid.astype(F32)).astype(BF16)
    placed = jnp.dot(chosen, hi, preferred_element_type=F32)
    placed = placed + jnp.dot(chosen, mid, preferred_element_type=F32)
    placed = placed + jnp.dot(chosen, low, preferred_element_type=F32)
    p[...] = placed

    def chunk(k):
        return pl.ds(pl.multiple_of(k * 32, 32), 32)

    def all_of(buffer, send, recv):
        return remote(buffer, buffer, send, recv, other)

    for k in range(1, 8):
        remote(p.at[chunk((z + k) % 8)], sz.at[k - 1], rzs, rzr, z_peers[k - 1]).start()

    @pl.when(is_head)
    def _():
        to_other.wait_recv()
        for i in sent_blocks + (3, 7):
            block = head_block(i)
            out[i] = hg[block] + tin[block // 2, block % 2].T
            if i % 4 < 3:
                head_x(i, out.at[i]).start()

    @pl.when(is_next)
    def _():
        for i in (3, 7):
            out[i] = hg[head_block(i)]

    def x_total(c):
        acc = out[4 * c + 3]
        for k in range(3):
            head_x(4 * c + k, out.at[4 * c + k]).wait_recv()
            acc = acc + fin[c, k]
        return acc

    all_of(sz, rzs, rzr).wait_recv()
    acc = p[chunk(z), :]
    for k in range(7):
        acc = acc + sz[k]
    fz[0] = acc
    for k in range(1, 8):
        remote(fz.at[0], fz.at[k], bys, byr, y_peers[k - 1]).start()


    all_of(fz.at[pl.ds(1, 7)], bys, byr).wait_recv()
    acc = fz[(y + 8) % 8]
    for i in range(1, 8):
        acc = acc + fz[(y - i + 8) % 8]
    slab = x * 256
    at_z = pl.ds(pl.multiple_of(slab + z * 32, 32), 32)
    full[at_z, :] = acc

    def third_z(k):
        return remote(full.at[at_z], full.at[at_z], azs.at[k - 1], azr.at[k - 1], z_peers[k - 1])

    def third_z_in(k):
        src = pl.ds(pl.multiple_of(slab + ((z - k + 8) % 8) * 32, 32), 32)
        return remote(full.at[src], full.at[src], azs.at[k - 1], azr.at[k - 1], z_peers[k - 1])

    for k in range(1, 8):
        third_z(k).start()

    @pl.when(is_head)
    def _():
        for k in range(1, 4):
            tail_x(k).wait_recv()
        for c, parity in ((0, q_down), (1, 1 - q_down)):
            tsend[c] = tg[x, parity] + tfin[0, parity] + tfin[1, parity] + tfin[2, parity]
        tail_y(0, near_dev).start()
        tail_y(1, far_dev).start()

    ysend[...] = x_total(0)
    along_y = remote(ysend, yrecv, ps, pr, pair)
    along_y.start()

    def whole(xx):
        return pl.ds(pl.multiple_of(xx * 256, 256), 256)

    def spread(n):
        at = full.at[pl.ds(pl.multiple_of(slab + n * 32, 32), 32)]
        for k in (1, 3, 2):
            remote(at, at, gxs.at[k - 1], gxr.at[k - 1], x_peers[k - 1]).start()

    def gather_x_all(k):
        at = full.at[whole((x - k + 4) % 4)]
        return remote(at, at, gxs.at[k - 1], gxr.at[k - 1], x_peers[k - 1])

    def swap(k):
        at = whole((x - k + 4) % 4)
        return remote(full.at[at], peer.at[at], gcs.at[k], gcr.at[k], other)

    spread(z)
    for k in (1, 7, 2, 6, 3, 5, 4):
        third_z_in(k).wait_recv()
        spread((z - k + 8) % 8)
    swap(0).start()
    ent[...] = x_total(1)
    along_y.wait_recv()
    ent[...] += yrecv[...]

    @pl.when(is_next)
    def _():
        for c in range(2):
            tail_y(c, near_dev).wait_recv()
        ent[...] += (trecv[0] + trecv[1]).T

    for k in (1, 3, 2):
        gather_x_all(k).wait_recv()
        swap(k).start()

    n = rel.shape[0]

    @pl.when(is_head)
    def _():
        rel[:, 0:128] = full[0:n, :]

    @pl.when(is_next)
    def _():
        rel[:, 128:256] = full[0:n, :]

    for k in range(4):
        swap(k).wait_recv()

    @pl.when(is_head)
    def _():
        rel[:, 128:256] = peer[0:n, :]

    @pl.when(is_next)
    def _():
        rel[:, 0:128] = peer[0:n, :]

    seven.wait_send()
    for i in sent_blocks:
        head_x(i, out.at[i]).wait_send()

    @pl.when(is_head)
    def _():
        for k in range(1, 4):
            tail_x(k).wait_send()
        for c in range(2):
            tail_y(c, near_dev).wait_send()

    @pl.when(is_next)
    def _():
        to_other.wait_send()

    for k in range(1, 8):
        third_z(k).wait_send()
    all_of(sz, rzs, rzr).wait_send()
    all_of(fz.at[pl.ds(1, 7)], bys, byr).wait_send()
    along_y.wait_send()
    for k in range(1, 4):
        gather_x_all(k).wait_send()
    for k in range(4):
        swap(k).wait_send()


def reduce(hg, tg, listed, relations):
    whole = pl.BlockSpec(memory_space=VMEM)
    dma = pltpu.SemaphoreType.DMA
    rows = listed.shape[1]
    return pl.pallas_call(
        reduce_kernel,
        name="reduce_gradients",
        out_shape=(jax.ShapeDtypeStruct((BLOCK, WIDTH), F32), jax.ShapeDtypeStruct((relations, WIDTH), F32)),
        in_specs=[whole] * 3,
        out_specs=(whole, whole),
        scratch_shapes=[
            VMEM((8, rows, 128), F32),
            VMEM((4, 2, WIDTH, BLOCK), F32),
            VMEM((BLOCKS, BLOCK, WIDTH), F32),
            VMEM((2, 3, BLOCK, WIDTH), F32),
            VMEM((3, 2, WIDTH, BLOCK), F32),
            VMEM((2, WIDTH, BLOCK), F32),
            VMEM((2, WIDTH, BLOCK), F32),
            VMEM((BLOCK, WIDTH), F32),
            VMEM((BLOCK, WIDTH), F32),
            VMEM((256, 128), F32),
            VMEM((7, 32, 128), F32),
            VMEM((8, 32, 128), F32),
            VMEM((REL_PAD, 128), F32),
            VMEM((REL_PAD, 128), F32),
            dma, dma,
            dma, dma,
            dma((8,)), dma((8,)),
            dma((3,)), dma((3,)),
            dma((2,)), dma((2,)),
            dma, dma,
            dma, dma, dma, dma,
            dma((7,)), dma((7,)),
            dma((3,)), dma((3,)),
            dma((4,)), dma((4,)),
        ],
        compiler_params=pltpu.CompilerParams(collective_id=1, has_side_effects=True, vmem_limit_bytes=40 << 20),
    )(hg, tg, listed)


def local(entity, rel_weight, tile_rel, tile_head, tile_tail, tile_mask, negatives, tile_count):
    ready = gather(entity, rel_weight, negatives, tile_mask, tile_rel, tile_head, tile_tail)
    hg, tg, listed = terms(*ready, tile_count)
    return reduce(hg, tg, listed, rel_weight.shape[0])


def solution(mesh):
    return jax.shard_map(
        local,
        mesh=mesh,
        in_specs=(
            P(("shard", "rep"), None),
            P(),
            P(("shard", "rep")),
            P(("shard", "rep")),
            P(("shard", "rep")),
            P(("shard", "rep"), None, None),
            P(("shard", "rep"), None),
            P(("shard", "rep")),
        ),
        out_specs=(P(("shard", "rep"), None), P()),
        check_vma=False,
    )
```
